32 devices in a mesh: copies: 2 (over y), blk: 4 (over x, core), virt: 4 (over z).
Axes of the slice: x: 2, y: 2, z: 4, core: 2. Of those that a mesh axis runs over, the one named last changes fastest.
Arguments:
- three_index: bfloat16 [32, 512, 2048], P(('copies', 'blk'), 'virt'), parts along dimension 0, may hold values from -0.59765625 to 0.59765625
- occ_energy: float32 [32], P(('copies', 'blk')), parts along dimension 0, may hold values from -2 to -0.5
- virt_energy: float32 [1024], P('copies'), parts along dimension 0, may hold values from 0.3 to 3
Outputs:
- gradient: bfloat16 [32, 512, 2048], P(('copies', 'blk'), 'virt'), parts along dimension 0
The draws below stay inside these ranges and needn't reach their ends.
There are 2 independent parts, one for each index of `copies`. The reference program is written for one: setup_inputs(seed, part) draws one part's arguments, and reference() takes and returns one part's arrays. A program takes and returns all parts, laid end to end along the dimension named above; each array names one. Nothing has to cross between parts.
All inputs are finite; a program needn't handle non-finite values.
Results may differ from the reference program's by a relative error of at most 0.0055.
Values may be sent and summed in bfloat16 or wider, within the bound.
A program may use at most 64 MiB of HBM per device.

```python
import jax
import jax.numpy as jnp
from jax import lax

OCC_BLK = 4
VIRT = 512
AUX = 2048
NOCC = 16
N_BLK = 4


def level_of(own_key, shape, cuts, smallest, largest):
    loudness = 1.0
    for position, parts in cuts:
        heights = jax.random.uniform(jax.random.fold_in(jax.random.fold_in(own_key, 6), position), (parts,), jnp.float32, smallest / len(cuts), largest / len(cuts))
        loudness = loudness * jnp.repeat(jnp.exp(heights), shape[position] // parts).reshape((-1,) + (1,) * (len(shape) - 1 - position))
    return loudness


def bell_draw(stream_key, dims, width, reach, cuts=(), kind=jnp.bfloat16):
    drawn = width * jax.random.normal(stream_key, dims, jnp.float32)
    if cuts:
        drawn = drawn * level_of(stream_key, dims, cuts, -0.22, 0.18)
    return jnp.clip(drawn, -reach, reach).astype(kind)


def setup_inputs(seed: int = 0, part: int = 0) -> dict:
    key_list = jax.random.split(jax.random.key(seed), 4)
    own_keys = jax.random.split(jax.random.fold_in(key_list[3], part), 4)
    return {
        "three_index": bell_draw(own_keys[0], (NOCC, VIRT, AUX), 0.1, 0.59765625, ((0, 4), (1, 4))),
        "occ_energy": jnp.clip(-2.0 + 1.5 * jax.random.uniform(own_keys[1], (NOCC,), jnp.float32) ** level_of(own_keys[1], (NOCC,), ((0, 4),), -0.2, 0.2), -2.0, -0.5),
        "virt_energy": jnp.clip(jax.random.uniform(own_keys[2], (VIRT,), jnp.float32, 0.3, 3.0), 0.3, 3.0),
    }


def pair_terms(block_own, block_part, energy_own, energy_part, virt_energy):
    occ_count, virt_count, aux_count = block_own.shape
    first = jnp.dot(block_own.reshape(occ_count * virt_count, aux_count), block_part.reshape(occ_count * virt_count, aux_count).T, preferred_element_type=jnp.float32)
    first = first.reshape(occ_count, virt_count, occ_count, virt_count)
    swapped = first.transpose(0, 3, 2, 1)
    denom = energy_own[:, None, None, None] + energy_part[None, None, :, None] - virt_energy[None, :, None, None] - virt_energy[None, None, None, :]
    tbar = ((2.0 * first - swapped) / denom).astype(jnp.bfloat16)
    flat = tbar.reshape(occ_count * virt_count, occ_count * virt_count)
    own = jnp.dot(flat, block_part.reshape(occ_count * virt_count, aux_count), preferred_element_type=jnp.float32)
    return flat, own.reshape(occ_count, virt_count, aux_count)


def partner_term(flat, block_own):
    occ_count, virt_count, aux_count = block_own.shape
    total = lax.dot_general(flat, block_own.reshape(occ_count * virt_count, aux_count), (((0,), (0,)), ((), ())), preferred_element_type=jnp.float32)
    return total.reshape(occ_count, virt_count, aux_count).astype(jnp.bfloat16)


def reference(three_index, occ_energy, virt_energy):
    owns = []
    partners = []
    for group in range(N_BLK):
        other = (group - 1) % N_BLK
        block_own = three_index[group * OCC_BLK:(group + 1) * OCC_BLK]
        block_part = three_index[other * OCC_BLK:(other + 1) * OCC_BLK]
        energy_own = occ_energy[group * OCC_BLK:(group + 1) * OCC_BLK]
        energy_part = occ_energy[other * OCC_BLK:(other + 1) * OCC_BLK]
        unused, diag_own = pair_terms(block_own, block_own, energy_own, energy_own, virt_energy)
        flat, cross_own = pair_terms(block_own, block_part, energy_own, energy_part, virt_energy)
        owns.append(diag_own + cross_own)
        partners.append(partner_term(flat, block_own))
    blocks = []
    for group in range(N_BLK):
        later = (group + 1) % N_BLK
        blocks.append((owns[group] + partners[later].astype(jnp.float32)).astype(jnp.bfloat16))
    return jnp.concatenate(blocks, axis=0)
```

```python
import functools

import jax
import jax.numpy as jnp
from jax import lax
from jax.experimental import pallas as pl
from jax.experimental.pallas import tpu as pltpu
from jax.sharding import PartitionSpec as P

MESH = pl.DeviceIdType.MESH
SEND_COLUMNS = 256
SUM_COLUMNS = 1024


def shifted(shard, axis, by):
    devices = lax.axis_size(axis)
    return lax.ppermute(shard, axis, [(i, (i + by) % devices) for i in range(devices)])


def contract(left, right):
    return lax.dot_general(
        left, right, (((1,), (1,)), ((), ())), preferred_element_type=jnp.float32
    )


def plain_local(three_index, occ_energy, virt_energy):
    occ, rows, aux = three_index.shape
    virt = virt_energy.shape[0]
    energy_rows = lax.dynamic_slice_in_dim(virt_energy, lax.axis_index("virt") * rows, rows, 0)
    part_rows = shifted(three_index, "blk", 1)
    own_full = lax.all_gather(three_index, "virt", axis=1, tiled=True)
    part_full = shifted(own_full, "blk", 1)
    energy_part = shifted(occ_energy, "blk", 1)

    def pairs(left, right):
        both = contract(left.reshape(occ * rows, aux), right.reshape(occ * virt, aux))
        return both.reshape(occ, rows, occ, virt)

    def denominator(left, right):
        return (
            left[:, None, None, None]
            + right[None, None, :, None]
            - energy_rows[None, :, None, None]
            - virt_energy[None, None, None, :]
        )

    def spread(tbar, full):
        return jnp.dot(
            tbar.astype(jnp.bfloat16).reshape(occ * rows, occ * virt),
            full.reshape(occ * virt, aux),
            preferred_element_type=jnp.float32,
        ).reshape(occ, rows, aux)

    diag = pairs(three_index, own_full)
    first = pairs(three_index, part_full)
    second = pairs(part_rows, own_full)
    own = spread(
        (2.0 * diag - diag.transpose(2, 1, 0, 3)) / denominator(occ_energy, occ_energy), own_full
    )
    own += spread(
        (2.0 * first - second.transpose(2, 1, 0, 3)) / denominator(occ_energy, energy_part),
        part_full,
    )
    partner = spread(
        (2.0 * second - first.transpose(2, 1, 0, 3)) / denominator(energy_part, occ_energy),
        own_full,
    ).astype(jnp.bfloat16)
    partner = shifted(partner, "blk", -1)
    return (own + partner.astype(jnp.float32)).astype(jnp.bfloat16)


def kernel(
    blocks,
    a_ref,
    e_ref,
    row_ref,
    o_ref,
    own_full,
    part_full,
    near,
    e_part,
    column_ref,
    tot,
    ptot,
    psend,
    precv,
    hsend,
    hrecv,
    rsend,
    rrecv,
    rel,
    k_ref,
    x_ref,
    td_ref,
    tu_ref,
    t_ref,
    staged,
    send_in,
    send_out,
    send_next,
    send_part,
    recv_own,
    recv_part,
    side_sems,
    pass_sems,
    back_sems,
    help_sems,
    result_sems,
    rel_sems,
    e_sems,
    out_sems,
    local_sem,
):
    occ, rows, aux = a_ref.shape
    size = occ * rows
    half = aux // 2
    cuts = 2 * occ
    parts = aux // SEND_COLUMNS
    chunks = range(parts)
    v = lax.axis_index("virt")
    g = lax.axis_index("blk")
    copy = lax.axis_index("copies")
    other = 1 - copy
    after = lax.rem(g + 1, blocks)
    before = lax.rem(g + blocks - 1, blocks)
    middle = (v == 1) | (v == 2)
    end = (v == 0) | (v == 3)
    even = lax.rem(g, 2) == 0
    full = copy == 0
    lean = copy == 1
    adj = v + 1 - 2 * lax.rem(v, 2)
    mid = jnp.where(v < 2, 2, 1)
    tip = jnp.where(v < 2, 3, 0)
    inner = jnp.where(middle, mid, adj)
    helper = middle & lean
    served = end & lean
    gathers = jnp.logical_not(served)

    def remote(src, dst, send, recv, **where):
        return pltpu.make_async_remote_copy(
            src_ref=src, dst_ref=dst, send_sem=send, recv_sem=recv,
            device_id=where, device_id_type=MESH,
        )

    def piece(ref, *lead):
        *lead, c = lead
        if isinstance(c, int):
            i, cols = c // 2, slice((c % 2) * half, (c % 2 + 1) * half)
        else:
            i, cols = c // 2, pl.ds(pl.multiple_of(lax.rem(c, 2) * half, half), half)
        return ref.at[(*lead, i, slice(None), cols)]

    def to_inner(s, c):
        return remote(
            piece(own_full, s, c), piece(own_full, s, c), send_in.at[s, c], recv_own.at[s, c], virt=inner
        )

    def to_outer(s, c):
        return remote(
            piece(own_full, s, c), piece(own_full, s, c), send_out.at[s, c], recv_own.at[s, c], virt=adj
        )

    def to_next(s, c):
        return remote(
            piece(own_full, s, c), piece(part_full, s, c), send_next.at[s, c], recv_part.at[s, c],
            blk=after,
        )

    def part_to_inner(c):
        return remote(
            piece(part_full, v, c), piece(part_full, v, c), send_part.at[c], recv_part.at[v, c],
            virt=adj,
        )

    def own_inner(c):
        return remote(
            piece(a_ref, c), piece(own_full, v, c), send_in.at[v, c], recv_own.at[v, c], virt=inner
        )

    def own_next(c):
        return remote(
            piece(a_ref, c), piece(part_full, v, c), send_next.at[v, c], recv_part.at[v, c], blk=after
        )

    def own_side(c):
        return remote(
            piece(a_ref, c), piece(near, c), side_sems.at[0, c], side_sems.at[1, c], copies=other
        )

    def pass_side(c):
        return remote(
            piece(near, c), piece(own_full, v, c), pass_sems.at[c], recv_own.at[v, c],
            copies=other, virt=adj,
        )

    def back(k):
        return remote(
            psend.at[k], precv.at[k], back_sems.at[0, k], back_sems.at[1, k], blk=before
        )

    def help_back(k):
        return remote(
            hsend.at[k], hrecv.at[k], help_sems.at[0, k], help_sems.at[1, k], blk=before
        )

    def by_side(k):
        return k % 2 == 1

    def result(k):
        if by_side(k):
            return remote(
                rsend.at[k], rel.at[k // 2], result_sems.at[0, k], rel_sems.at[0, k // 2], copies=other
            )
        return remote(
            rsend.at[k], rrecv.at[k], result_sems.at[0, k], result_sems.at[1, k], virt=adj
        )

    def pass_result(k):
        return remote(
            rel.at[k // 2], rrecv.at[k], rel_sems.at[1, k // 2], result_sems.at[1, k],
            copies=other, virt=adj,
        )

    def write(k):
        cols = slice(k * SEND_COLUMNS, (k + 1) * SEND_COLUMNS)
        return pltpu.make_async_copy(staged.at[k], o_ref.at[:, :, cols], out_sems.at[k])

    energy_copy = remote(e_ref, e_part, e_sems.at[0], e_sems.at[1], blk=after)
    keep = pltpu.make_async_copy(a_ref, own_full.at[v], local_sem)

    barrier = pltpu.get_barrier_semaphore()
    pl.semaphore_signal(barrier, inc=1, device_id={"blk": after}, device_id_type=MESH)
    pl.semaphore_signal(barrier, inc=1, device_id={"blk": before}, device_id_type=MESH)
    pl.semaphore_signal(barrier, inc=1, device_id={"virt": adj}, device_id_type=MESH)
    pl.semaphore_signal(barrier, inc=1, device_id={"copies": other, "virt": adj}, device_id_type=MESH)

    @pl.when(middle)
    def _():
        pl.semaphore_signal(barrier, inc=1, device_id={"virt": mid}, device_id_type=MESH)
        pl.semaphore_signal(barrier, inc=1, device_id={"copies": other}, device_id_type=MESH)

    pl.semaphore_wait(barrier, 4 + 2 * middle.astype(jnp.int32))

    for c in range(cuts):
        own_inner(c).start()

        @pl.when(middle & full)
        def _():
            own_side(c).start()

    energy_copy.start()
    for c in range(cuts):
        own_next(c).start()
    keep.start()
    for s in range(4):
        column_ref[s] = jnp.transpose(jnp.broadcast_to(row_ref[s], (rows, rows)))[:, 0:1]
    for w in range(2):
        @pl.loop(0, aux // SEND_COLUMNS)
        def _(k):
            cols = pl.ds(pl.multiple_of(k * SEND_COLUMNS, SEND_COLUMNS), SEND_COLUMNS)
            tot[w, :, cols] = jnp.zeros((size, SEND_COLUMNS), jnp.float32)
            ptot[w, :, cols] = jnp.zeros((size, SEND_COLUMNS), jnp.float32)

    keep.wait()

    def inverse(left, i, right, j, r, s):
        return 1.0 / (
            (left[0:1, i : i + 1] + right[0:1, j : j + 1]) - column_ref[r] - row_ref[s]
        )

    def at(i):
        return slice(i * rows, (i + 1) * rows)

    def product(left, source, s, cols, width):
        return jnp.dot(
            left[...], source[s, :, :, cols].reshape(size, width),
            preferred_element_type=jnp.float32,
        )

    def add_columns(total, w, left, source, s):
        @pl.loop(0, aux // SUM_COLUMNS)
        def _(k):
            cols = pl.ds(pl.multiple_of(k * SUM_COLUMNS, SUM_COLUMNS), SUM_COLUMNS)
            total[w, :, cols] += product(left, source, s, cols, SUM_COLUMNS)

    def shard(source, s):
        return source[s].reshape(size, aux)

    def part_arrives(s):
        for c in range(cuts):
            to_next(s, c).wait_recv()

    def pair_ratio(r, s):
        k_ref[...] = contract(shard(own_full, r), shard(own_full, s))
        for i in range(occ):
            for j in range(occ):
                td_ref[at(i), at(j)] = (
                    (2.0 * k_ref[at(i), at(j)] - k_ref[at(j), at(i)])
                    * inverse(e_ref, i, e_ref, j, r, s)
                ).astype(jnp.bfloat16)

    def diagonal(r, s, w):
        pair_ratio(r, s)
        add_columns(tot, w, td_ref, own_full, s)

    def cross(r, s):
        k_ref[...] = contract(shard(part_full, r), shard(own_full, s))
        x_ref[...] = contract(shard(own_full, r), shard(part_full, s))
        for i in range(occ):
            for j in range(occ):
                scale = inverse(e_ref, i, e_part, j, r, s)
                x = x_ref[at(i), at(j)]
                y = k_ref[at(j), at(i)]
                t_ref[at(i), at(j)] = ((2.0 * x - y) * scale).astype(jnp.bfloat16)
                tu_ref[at(j), at(i)] = ((2.0 * y - x) * scale).astype(jnp.bfloat16)

    def spread(s, w):
        add_columns(ptot, w, tu_ref, own_full, s)
        add_columns(tot, w, t_ref, part_full, s)

    def first_half(c):
        @pl.when(gathers)
        def _():
            to_inner(mid, c).wait_recv()

            @pl.when(middle & full)
            def _():
                to_outer(mid, c).start()

            to_next(mid, c).start()

            @pl.when(middle)
            def _():
                to_inner(adj, c).wait_recv()
                to_inner(adj, c).start()

                @pl.when(even)
                def _():
                    to_next(adj, c).start()

            @pl.when(helper)
            def _():
                own_side(c).wait_recv()
                pass_side(c).start()

            @pl.when(end)
            def _():
                to_inner(adj, c).wait_recv()
                to_next(adj, c).start()

    def second_half(c):
        to_inner(tip, c).wait_recv()

        @pl.when(middle)
        def _():
            to_outer(tip, c).start()

        to_next(tip, c).start()

    def send_help(k):
        cols = slice(k * SEND_COLUMNS, (k + 1) * SEND_COLUMNS)
        hsend[k] = ptot[1, :, cols].astype(jnp.bfloat16)
        help_back(k).start()

    def send_result(k):
        cols = slice(k * SEND_COLUMNS, (k + 1) * SEND_COLUMNS)
        help_back(k).wait_recv()
        rsend[k] = (tot[1, :, cols] + hrecv[k].astype(jnp.float32)).astype(jnp.bfloat16)
        result(k).start()

    EARLY = 3
    pair_ratio(v, v)
    first_half(0)
    add_columns(tot, 0, td_ref, own_full, v)
    energy_copy.wait_recv()
    first_half(1)
    first_half(2)
    part_arrives(v)

    @pl.when(end & even)
    def _():
        for c in range(cuts):
            part_to_inner(c).start()

    first_half(3)
    cross(v, v)
    spread(v, 0)

    @pl.loop(4, cuts)
    def _(c):
        first_half(c)

    steps = jnp.where(helper, 5, jnp.where(full, 3, 1))

    @pl.loop(1, steps)
    def _(t):
        assist = helper & ((t == 2) | (t == 3))
        r = jnp.where(assist, adj, v)
        s = jnp.where(t == 1, mid, jnp.where(helper, jnp.where(t == 2, mid, jnp.where(t == 3, v, adj)), adj))
        w = assist.astype(jnp.int32)
        diagonal(r, s, w)
        second_half(2 * t - 2)

        @pl.when(t == 1)
        def _():
            part_arrives(mid)

        @pl.when(t == 2)
        def _():
            part_arrives(adj)

        cross(r, s)
        second_half(2 * t - 1)
        spread(s, w)

        @pl.when(helper & (t == 3))
        def _():
            for k in range(EARLY):
                send_help(k)

    @pl.loop(2 * steps - 2, cuts)
    def _(c):
        second_half(c)

    @pl.when(helper)
    def _():
        for k in range(EARLY, parts):
            send_help(k)
        for k in range(EARLY):
            send_result(k)

    pair_ratio(v, tip)
    part_arrives(tip)
    cross(v, tip)
    for k in chunks:
        cols = slice(k * SEND_COLUMNS, (k + 1) * SEND_COLUMNS)
        psend[k] = (
            ptot[0, :, cols] + product(tu_ref, own_full, tip, cols, SEND_COLUMNS)
        ).astype(jnp.bfloat16)
        back(k).start()

        @pl.when(helper)
        def _():
            if k + EARLY < parts:
                send_result(k + EARLY)

        if by_side(k):
            @pl.when(middle & full)
            def _():
                result(k).wait_recv()
                pass_result(k).start()

    add_columns(tot, 0, td_ref, own_full, tip)
    add_columns(tot, 0, t_ref, part_full, tip)
    for k in chunks:
        cols = slice(k * SEND_COLUMNS, (k + 1) * SEND_COLUMNS)

        @pl.when(served)
        def _():
            pass_result(k).wait_recv()
            tot[0, :, cols] += rrecv[k].astype(jnp.float32)

        back(k).wait_recv()
        staged[k] = (
            (tot[0, :, cols] + precv[k].astype(jnp.float32))
            .astype(jnp.bfloat16)
            .reshape(occ, rows, SEND_COLUMNS)
        )
        write(k).start()

    energy_copy.wait_send()
    for k in chunks:
        back(k).wait_send()
        write(k).wait()

    @pl.loop(0, cuts)
    def _(c):
        to_inner(v, c).wait_send()
        to_next(v, c).wait_send()
        to_next(tip, c).wait_send()

        @pl.when(gathers)
        def _():
            to_next(mid, c).wait_send()

        @pl.when(middle)
        def _():
            to_inner(adj, c).wait_send()
            to_outer(tip, c).wait_send()

        @pl.when((middle & even) | (end & full))
        def _():
            to_next(adj, c).wait_send()

        @pl.when(middle & full)
        def _():
            to_outer(mid, c).wait_send()
            own_side(c).wait_send()

        @pl.when(helper)
        def _():
            pass_side(c).wait_send()

        @pl.when(end & even)
        def _():
            part_to_inner(c).wait_send()

    @pl.when(helper)
    def _():
        for k in chunks:
            help_back(k).wait_send()
            result(k).wait_send()

    @pl.when(middle & full)
    def _():
        for k in chunks:
            if by_side(k):
                pass_result(k).wait_send()


def fused_local(three_index, occ_energy, virt_energy):
    occ, rows, aux = three_index.shape
    members, blocks = lax.axis_size("virt"), lax.axis_size("blk")
    size, parts = occ * rows, aux // SEND_COLUMNS
    vmem = pl.BlockSpec(memory_space=pltpu.VMEM)
    dma = pltpu.SemaphoreType.DMA
    full = pltpu.VMEM((members, occ, rows, aux), jnp.bfloat16)
    total = pltpu.VMEM((2, size, aux), jnp.float32)
    pieces = pltpu.VMEM((parts, size, SEND_COLUMNS), jnp.bfloat16)
    return pl.pallas_call(
        functools.partial(kernel, blocks),
        out_shape=jax.ShapeDtypeStruct((occ, rows, aux), jnp.bfloat16),
        in_specs=[pl.BlockSpec(memory_space=pl.ANY), vmem, vmem],
        out_specs=pl.BlockSpec(memory_space=pl.ANY),
        scratch_shapes=[
            full,
            full,
            pltpu.VMEM((occ, rows, aux), jnp.bfloat16),
            pltpu.VMEM((1, occ), jnp.float32),
            pltpu.VMEM((members, rows, 1), jnp.float32),
            *[total] * 2,
            *[pieces] * 6,
            pltpu.VMEM((parts // 2, size, SEND_COLUMNS), jnp.bfloat16),
            *[pltpu.VMEM((size, size), jnp.float32)] * 2,
            *[pltpu.VMEM((size, size), jnp.bfloat16)] * 3,
            pltpu.VMEM((parts, occ, rows, SEND_COLUMNS), jnp.bfloat16),
            *[dma((members, 2 * occ))] * 3,
            dma((2 * occ,)),
            *[dma((members, 2 * occ))] * 2,
            dma((2, 2 * occ)),
            dma((2 * occ,)),
            *[dma((2, parts))] * 3,
            dma((2, parts // 2)),
            dma((2,)),
            dma((parts,)),
            dma,
        ],
        compiler_params=pltpu.CompilerParams(
            collective_id=0, has_side_effects=True, vmem_limit_bytes=63 * 2**20
        ),
    )(three_index, occ_energy.reshape(1, occ), virt_energy.reshape(members, 1, rows))


def local(three_index, occ_energy, virt_energy):
    occ, rows, aux = three_index.shape
    tiles = rows % 128 == 0 and aux % SUM_COLUMNS == 0 and occ >= 4
    pairs = lax.axis_size("copies") == 2 and lax.axis_size("blk") % 2 == 0
    if tiles and pairs and lax.axis_size("virt") == 4:
        return fused_local(three_index, occ_energy, virt_energy)
    return plain_local(three_index, occ_energy, virt_energy)


def solution(mesh):
    placed = (P(("copies", "blk"), "virt", None), P(("copies", "blk")), P("copies"))
    return jax.shard_map(
        local,
        mesh=mesh,
        in_specs=placed,
        out_specs=P(("copies", "blk"), "virt", None),
        check_vma=False,
    )
```

```python
import functools

import jax
import jax.numpy as jnp
from jax import lax
from jax.experimental import pallas as pl
from jax.experimental.pallas import tpu as pltpu
from jax.sharding import PartitionSpec as P

MESH = pl.DeviceIdType.MESH
SEND_COLUMNS = 256
SUM_COLUMNS = 1024
STRIPS = 2
READY = 3
PACE = (2, 3, 4, 5, 6, 7, 8)


def shifted(shard, axis, by):
    devices = lax.axis_size(axis)
    return lax.ppermute(shard, axis, [(i, (i + by) % devices) for i in range(devices)])


def contract(left, right):
    return lax.dot_general(
        left, right, (((1,), (1,)), ((), ())), preferred_element_type=jnp.float32
    )


def plain_local(three_index, occ_energy, virt_energy):
    occ, rows, aux = three_index.shape
    virt = virt_energy.shape[0]
    energy_rows = lax.dynamic_slice_in_dim(virt_energy, lax.axis_index("virt") * rows, rows, 0)
    part_rows = shifted(three_index, "blk", 1)
    own_full = lax.all_gather(three_index, "virt", axis=1, tiled=True)
    part_full = shifted(own_full, "blk", 1)
    energy_part = shifted(occ_energy, "blk", 1)

    def pairs(left, right):
        both = contract(left.reshape(occ * rows, aux), right.reshape(occ * virt, aux))
        return both.reshape(occ, rows, occ, virt)

    def denominator(left, right):
        return (
            left[:, None, None, None]
            + right[None, None, :, None]
            - energy_rows[None, :, None, None]
            - virt_energy[None, None, None, :]
        )

    def spread(tbar, full):
        return jnp.dot(
            tbar.astype(jnp.bfloat16).reshape(occ * rows, occ * virt),
            full.reshape(occ * virt, aux),
            preferred_element_type=jnp.float32,
        ).reshape(occ, rows, aux)

    diag = pairs(three_index, own_full)
    first = pairs(three_index, part_full)
    second = pairs(part_rows, own_full)
    own = spread(
        (2.0 * diag - diag.transpose(2, 1, 0, 3)) / denominator(occ_energy, occ_energy), own_full
    )
    own += spread(
        (2.0 * first - second.transpose(2, 1, 0, 3)) / denominator(occ_energy, energy_part),
        part_full,
    )
    partner = spread(
        (2.0 * second - first.transpose(2, 1, 0, 3)) / denominator(energy_part, occ_energy),
        own_full,
    ).astype(jnp.bfloat16)
    partner = shifted(partner, "blk", -1)
    return (own + partner.astype(jnp.float32)).astype(jnp.bfloat16)


def kernel(
    blocks,
    a_ref,
    e_ref,
    row_ref,
    o_ref,
    own_full,
    part_full,
    near,
    e_part,
    column_ref,
    tot,
    ptot,
    psend,
    precv,
    hsend,
    hrecv,
    rsend,
    rrecv,
    rel,
    k_ref,
    x_ref,
    d_ref,
    td_ref,
    tu_ref,
    t_ref,
    send_in,
    send_out,
    send_next,
    send_part,
    recv_own,
    recv_part,
    side_sems,
    pass_sems,
    back_sems,
    help_sems,
    result_sems,
    rel_sems,
    e_sems,
    local_sem,
):
    occ, rows, aux = a_ref.shape
    size = occ * rows
    high = rows // STRIPS
    cuts = STRIPS * occ
    turn = cuts // 8
    direct = cuts // 2
    parts = aux // SEND_COLUMNS
    chunks = range(parts)
    v = lax.axis_index("virt")
    g = lax.axis_index("blk")
    copy = lax.axis_index("copies")
    other = 1 - copy
    after = lax.rem(g + 1, blocks)
    before = lax.rem(g + blocks - 1, blocks)
    middle = (v == 1) | (v == 2)
    end = (v == 0) | (v == 3)
    even = lax.rem(g, 2) == 0
    full = copy == 0
    lean = copy == 1
    adj = v + 1 - 2 * lax.rem(v, 2)
    mid = jnp.where(v < 2, 2, 1)
    tip = jnp.where(v < 2, 3, 0)
    inner = jnp.where(middle, mid, adj)
    helper = middle & lean
    served = end & lean
    gathers = jnp.logical_not(served)

    def remote(src, dst, send, recv, **where):
        return pltpu.make_async_remote_copy(
            src_ref=src, dst_ref=dst, send_sem=send, recv_sem=recv,
            device_id=where, device_id_type=MESH,
        )

    def piece(ref, *lead):
        *lead, c = lead
        if isinstance(c, int):
            i, first = c // STRIPS, (c % STRIPS) * high
        else:
            i = lax.div(c, STRIPS)
            first = pl.multiple_of(lax.rem(c, STRIPS) * high, high)
        return ref.at[(*lead, i, pl.ds(first, high))]

    def to_inner(s, c):
        return remote(
            piece(own_full, s, c), piece(own_full, s, c), send_in.at[s, c], recv_own.at[s, c], virt=inner
        )

    def to_outer(s, c):
        return remote(
            piece(own_full, s, c), piece(own_full, s, c), send_out.at[s, c], recv_own.at[s, c], virt=adj
        )

    def to_next(s, c):
        return remote(
            piece(own_full, s, c), piece(part_full, s, c), send_next.at[s, c], recv_part.at[s, c],
            blk=after,
        )

    def part_to_inner(c):
        return remote(
            piece(part_full, v, c), piece(part_full, v, c), send_part.at[c], recv_part.at[v, c],
            virt=adj,
        )

    def own_inner(c):
        return remote(
            piece(a_ref, c), piece(own_full, v, c), send_in.at[v, c], recv_own.at[v, c], virt=inner
        )

    def own_next(c):
        return remote(
            piece(a_ref, c), piece(part_full, v, c), send_next.at[v, c], recv_part.at[v, c], blk=after
        )

    def own_side(c):
        return remote(
            piece(a_ref, c), piece(near, c), side_sems.at[0, c], side_sems.at[1, c], copies=other
        )

    def pass_side(c):
        return remote(
            piece(near, c), piece(own_full, v, c), pass_sems.at[c], recv_own.at[v, c],
            copies=other, virt=adj,
        )

    def back(k):
        return remote(
            psend.at[k], precv.at[k], back_sems.at[0, k], back_sems.at[1, k], blk=before
        )

    def help_back(k):
        return remote(
            hsend.at[k], hrecv.at[k], help_sems.at[0, k], help_sems.at[1, k], blk=before
        )

    def by_side(k):
        return k % 2 == 1

    def result(k):
        if by_side(k):
            return remote(
                rsend.at[k], rel.at[k // 2], result_sems.at[0, k], rel_sems.at[0, k // 2], copies=other
            )
        return remote(
            rsend.at[k], rrecv.at[k], result_sems.at[0, k], result_sems.at[1, k], virt=adj
        )

    def pass_result(k):
        return remote(
            rel.at[k // 2], rrecv.at[k], rel_sems.at[1, k // 2], result_sems.at[1, k],
            copies=other, virt=adj,
        )

    energy_copy = remote(e_ref, e_part, e_sems.at[0], e_sems.at[1], blk=after)
    keep = pltpu.make_async_copy(a_ref, own_full.at[v], local_sem)

    barrier = pltpu.get_barrier_semaphore()
    pl.semaphore_signal(barrier, inc=1, device_id={"blk": after}, device_id_type=MESH)
    pl.semaphore_signal(barrier, inc=1, device_id={"blk": before}, device_id_type=MESH)
    pl.semaphore_signal(barrier, inc=1, device_id={"virt": adj}, device_id_type=MESH)
    pl.semaphore_signal(barrier, inc=1, device_id={"copies": other, "virt": adj}, device_id_type=MESH)

    @pl.when(middle)
    def _():
        pl.semaphore_signal(barrier, inc=1, device_id={"virt": mid}, device_id_type=MESH)
        pl.semaphore_signal(barrier, inc=1, device_id={"copies": other}, device_id_type=MESH)

    pl.semaphore_wait(barrier, 4 + 2 * middle.astype(jnp.int32))

    for c in range(cuts):
        own_inner(c).start()

        @pl.when(middle & full)
        def _():
            own_side(c).start()

    energy_copy.start()
    for c in range(cuts):
        own_next(c).start()
    keep.start()
    for s in range(4):
        column_ref[s] = jnp.transpose(jnp.broadcast_to(row_ref[s], (rows, rows)))[:, 0:1]
    for w in range(2):
        @pl.loop(0, aux // SEND_COLUMNS)
        def _(k):
            cols = pl.ds(pl.multiple_of(k * SEND_COLUMNS, SEND_COLUMNS), SEND_COLUMNS)
            tot[w, :, cols] = jnp.zeros((size, SEND_COLUMNS), jnp.float32)
            ptot[w, :, cols] = jnp.zeros((size, SEND_COLUMNS), jnp.float32)

    keep.wait()

    def inverse(left, i, right, j, r, s):
        return 1.0 / (
            (left[0:1, i : i + 1] + right[0:1, j : j + 1]) - column_ref[r] - row_ref[s]
        )

    def at(i):
        return slice(i * rows, (i + 1) * rows)

    def product(left, source, s, cols, width):
        return jnp.dot(
            left[...], source[s, :, :, cols].reshape(size, width),
            preferred_element_type=jnp.float32,
        )

    def add_columns(total, w, left, source, s):
        @pl.loop(0, aux // SUM_COLUMNS)
        def _(k):
            cols = pl.ds(pl.multiple_of(k * SUM_COLUMNS, SUM_COLUMNS), SUM_COLUMNS)
            total[w, :, cols] += product(left, source, s, cols, SUM_COLUMNS)

    def shard(source, s):
        return source[s].reshape(size, aux)

    def part_arrives(s):
        for c in range(cuts):
            to_next(s, c).wait_recv()

    def pair_ratio(r, s):
        k_ref[...] = contract(shard(own_full, r), shard(own_full, s))
        ratio(k_ref, r, s)

    def ratio(pairs, r, s):
        for i in range(occ):
            for j in range(occ):
                td_ref[at(i), at(j)] = (
                    (2.0 * pairs[at(i), at(j)] - pairs[at(j), at(i)])
                    * inverse(e_ref, i, e_ref, j, r, s)
                ).astype(jnp.bfloat16)

    def diagonal(r, s, w):
        pair_ratio(r, s)
        add_columns(tot, w, td_ref, own_full, s)

    def cross(r, s):
        k_ref[...] = contract(shard(part_full, r), shard(own_full, s))
        x_ref[...] = contract(shard(own_full, r), shard(part_full, s))
        amplitudes(r, s)

    def amplitudes(r, s, own=True, partner=True):
        for i in range(occ):
            for j in range(occ):
                scale = inverse(e_ref, i, e_part, j, r, s)
                x = x_ref[at(i), at(j)]
                y = k_ref[at(j), at(i)]
                if own:
                    t_ref[at(i), at(j)] = ((2.0 * x - y) * scale).astype(jnp.bfloat16)
                if partner:
                    tu_ref[at(j), at(i)] = ((2.0 * y - x) * scale).astype(jnp.bfloat16)

    def spread(s, w):
        add_columns(ptot, w, tu_ref, own_full, s)
        add_columns(tot, w, t_ref, part_full, s)

    def first_half(c):
        @pl.when(gathers)
        def _():
            to_inner(mid, c).wait_recv()

            @pl.when(middle & full)
            def _():
                to_outer(mid, c).start()

            to_next(mid, c).start()

            @pl.when(middle)
            def _():
                to_inner(adj, c).wait_recv()
                to_inner(adj, c).start()

                @pl.when(even | (c < direct))
                def _():
                    to_next(adj, c).start()

            @pl.when(helper)
            def _():
                own_side(c).wait_recv()
                pass_side(c).start()

            @pl.when(end)
            def _():
                to_inner(adj, c).wait_recv()
                to_next(adj, c).start()

    def second_half(c):
        to_inner(tip, c).wait_recv()

        @pl.when(middle)
        def _():
            to_outer(tip, c).start()

        to_next(tip, c).start()

    def send_help(k):
        cols = pl.ds(pl.multiple_of(k * SEND_COLUMNS, SEND_COLUMNS), SEND_COLUMNS)
        hsend[k] = ptot[1, :, cols].astype(jnp.bfloat16)
        help_back(k).start()

    def send_result(k):
        cols = slice(k * SEND_COLUMNS, (k + 1) * SEND_COLUMNS)
        help_back(k).wait_recv()
        rsend[k] = (tot[1, :, cols] + hrecv[k].astype(jnp.float32)).astype(jnp.bfloat16)
        result(k).start()

    def advance(handle, first, last):
        @pl.loop(first * turn, last * turn)
        def _(c):
            handle(c)

    pair_ratio(v, v)
    advance(first_half, 0, 1)
    add_columns(tot, 0, td_ref, own_full, v)
    energy_copy.wait_recv()
    advance(first_half, 1, 3)
    part_arrives(v)

    @pl.when(end & even)
    def _():
        for c in range(direct, cuts):
            part_to_inner(c).start()

    advance(first_half, 3, 4)
    cross(v, v)
    advance(first_half, 4, 5)
    spread(v, 0)
    advance(first_half, 5, 8)
    def paced(t, place):
        count = 0
        for index, sent in enumerate(PACE):
            count = jnp.where(3 * t + place >= 8 + index, sent, count)
        return jnp.where(helper, count, 0)

    def help_until(t, place):
        @pl.loop(paced(t, place - 1), paced(t, place))
        def _(k):
            send_help(k)

    steps = jnp.where(helper, 5, jnp.where(full, 3, 1))

    @pl.loop(1, steps)
    def _(t):
        assist = helper & (t < 3)
        r = jnp.where(assist, adj, v)
        s = jnp.where(
            helper, jnp.where(t == 2, v, jnp.where(t == 4, adj, mid)), jnp.where(t == 1, mid, adj)
        )
        w = assist.astype(jnp.int32)
        pairs = jnp.where(assist, jnp.where(t == 1, 2, 0), 1)

        @pl.loop(0, pairs)
        def _(d):
            diagonal(r, jnp.where(d == 1, v, s), w)

        advance(second_half, 2 * t - 2, 2 * t - 1)
        help_until(t, 0)

        @pl.when(t == 1)
        def _():
            part_arrives(mid)

        @pl.when(t == jnp.where(helper, 1, 2))
        def _():
            part_arrives(adj)

        cross(r, s)
        advance(second_half, 2 * t - 1, 2 * t)
        help_until(t, 1)
        spread(s, w)
        help_until(t, 2)

    ticks = 2 * steps - 2
    advance(second_half, ticks, 6)

    def own_pairs(h):
        block = own_full[tip, pl.ds(h * occ // 2, occ // 2)].reshape(size // 2, aux)
        columns = slice(h * size // 2, (h + 1) * size // 2)
        k_ref[:, columns] = contract(shard(part_full, v), block)
        d_ref[:, columns] = contract(shard(own_full, v), block)

    def part_pairs(h):
        for c in range(h * cuts // 2, (h + 1) * cuts // 2):
            to_next(tip, c).wait_recv()
        block = part_full[tip, pl.ds(h * occ // 2, occ // 2)].reshape(size // 2, aux)
        x_ref[:, slice(h * size // 2, (h + 1) * size // 2)] = contract(shard(own_full, v), block)

    own_pairs(0)
    advance(second_half, jnp.maximum(ticks, 6), 7)
    part_pairs(0)
    advance(second_half, jnp.maximum(ticks, 7), 8)

    @pl.when(helper)
    def _():
        for k in range(READY):
            send_result(k)

    own_pairs(1)
    ratio(d_ref, v, tip)
    part_pairs(1)
    amplitudes(v, tip, own=False)
    for k in chunks:
        cols = slice(k * SEND_COLUMNS, (k + 1) * SEND_COLUMNS)
        psend[k] = (
            ptot[0, :, cols] + product(tu_ref, own_full, tip, cols, SEND_COLUMNS)
        ).astype(jnp.bfloat16)
        back(k).start()

        @pl.when(helper)
        def _():
            if k + READY < parts:
                send_result(k + READY)

        if by_side(k):
            @pl.when(middle & full)
            def _():
                result(k).wait_recv()
                pass_result(k).start()

    amplitudes(v, tip, partner=False)
    add_columns(tot, 0, td_ref, own_full, tip)
    add_columns(tot, 0, t_ref, part_full, tip)
    for k in chunks:
        cols = slice(k * SEND_COLUMNS, (k + 1) * SEND_COLUMNS)

        @pl.when(served)
        def _():
            pass_result(k).wait_recv()
            tot[0, :, cols] += rrecv[k].astype(jnp.float32)

        back(k).wait_recv()
        o_ref[:, :, cols] = (
            (tot[0, :, cols] + precv[k].astype(jnp.float32))
            .astype(jnp.bfloat16)
            .reshape(occ, rows, SEND_COLUMNS)
        )

    energy_copy.wait_send()
    for k in chunks:
        back(k).wait_send()

    @pl.loop(0, cuts)
    def _(c):
        to_inner(v, c).wait_send()
        to_next(v, c).wait_send()
        to_next(tip, c).wait_send()

        @pl.when(gathers)
        def _():
            to_next(mid, c).wait_send()

        @pl.when(middle)
        def _():
            to_inner(adj, c).wait_send()
            to_outer(tip, c).wait_send()

        @pl.when((middle & (even | (c < direct))) | (end & full))
        def _():
            to_next(adj, c).wait_send()

        @pl.when(middle & full)
        def _():
            to_outer(mid, c).wait_send()
            own_side(c).wait_send()

        @pl.when(helper)
        def _():
            pass_side(c).wait_send()

        @pl.when(end & even & (c >= direct))
        def _():
            part_to_inner(c).wait_send()

    @pl.when(helper)
    def _():
        for k in chunks:
            help_back(k).wait_send()
            result(k).wait_send()

    @pl.when(middle & full)
    def _():
        for k in chunks:
            if by_side(k):
                pass_result(k).wait_send()


def fused_local(three_index, occ_energy, virt_energy):
    occ, rows, aux = three_index.shape
    members, blocks = lax.axis_size("virt"), lax.axis_size("blk")
    size, parts = occ * rows, aux // SEND_COLUMNS
    cuts = occ * STRIPS
    vmem = pl.BlockSpec(memory_space=pltpu.VMEM)
    dma = pltpu.SemaphoreType.DMA
    full = pltpu.VMEM((members, occ, rows, aux), jnp.bfloat16)
    total = pltpu.VMEM((2, size, aux), jnp.float32)
    pieces = pltpu.VMEM((parts, size, SEND_COLUMNS), jnp.bfloat16)
    return pl.pallas_call(
        functools.partial(kernel, blocks),
        out_shape=pltpu.VMEM((occ, rows, aux), jnp.bfloat16),
        in_specs=[pl.BlockSpec(memory_space=pl.ANY), vmem, vmem],
        out_specs=vmem,
        scratch_shapes=[
            full,
            full,
            pltpu.VMEM((occ, rows, aux), jnp.bfloat16),
            pltpu.VMEM((1, occ), jnp.float32),
            pltpu.VMEM((members, rows, 1), jnp.float32),
            *[total] * 2,
            *[pieces] * 6,
            pltpu.VMEM((parts // 2, size, SEND_COLUMNS), jnp.bfloat16),
            *[pltpu.VMEM((size, size), jnp.float32)] * 3,
            *[pltpu.VMEM((size, size), jnp.bfloat16)] * 3,
            *[dma((members, cuts))] * 3,
            dma((cuts,)),
            *[dma((members, cuts))] * 2,
            dma((2, cuts)),
            dma((cuts,)),
            *[dma((2, parts))] * 3,
            dma((2, parts // 2)),
            dma((2,)),
            dma,
        ],
        compiler_params=pltpu.CompilerParams(
            collective_id=0, has_side_effects=True, vmem_limit_bytes=58 * 2**20
        ),
    )(three_index, occ_energy.reshape(1, occ), virt_energy.reshape(members, 1, rows))


def local(three_index, occ_energy, virt_energy):
    occ, rows, aux = three_index.shape
    tiles = rows % 128 == 0 and aux % SUM_COLUMNS == 0 and occ >= 4
    paired = lax.axis_size("copies") == 2 and lax.axis_size("blk") % 2 == 0
    if tiles and paired and occ % 2 == 0 and lax.axis_size("virt") == 4:
        return fused_local(three_index, occ_energy, virt_energy)
    return plain_local(three_index, occ_energy, virt_energy)


def solution(mesh):
    placed = (P(("copies", "blk"), "virt", None), P(("copies", "blk")), P("copies"))
    return jax.shard_map(
        local,
        mesh=mesh,
        in_specs=placed,
        out_specs=P(("copies", "blk"), "virt", None),
        check_vma=False,
    )
```

```python
import functools

import jax
import jax.numpy as jnp
from jax import lax
from jax.experimental import pallas as pl
from jax.experimental.pallas import tpu as pltpu
from jax.sharding import PartitionSpec as P

MESH = pl.DeviceIdType.MESH
SEND_COLUMNS = 256
SUM_COLUMNS = 1024
STRIPS = 2
READY = 3
ASIDE = 3
PACE = (3, 4, 5, 5, 6, 7, 8)


def shifted(shard, axis, by):
    devices = lax.axis_size(axis)
    return lax.ppermute(shard, axis, [(i, (i + by) % devices) for i in range(devices)])


def contract(left, right):
    return lax.dot_general(
        left, right, (((1,), (1,)), ((), ())), preferred_element_type=jnp.float32
    )


def plain_local(three_index, occ_energy, virt_energy):
    occ, rows, aux = three_index.shape
    virt = virt_energy.shape[0]
    energy_rows = lax.dynamic_slice_in_dim(virt_energy, lax.axis_index("virt") * rows, rows, 0)
    part_rows = shifted(three_index, "blk", 1)
    own_full = lax.all_gather(three_index, "virt", axis=1, tiled=True)
    part_full = shifted(own_full, "blk", 1)
    energy_part = shifted(occ_energy, "blk", 1)

    def pairs(left, right):
        both = contract(left.reshape(occ * rows, aux), right.reshape(occ * virt, aux))
        return both.reshape(occ, rows, occ, virt)

    def denominator(left, right):
        return (
            left[:, None, None, None]
            + right[None, None, :, None]
            - energy_rows[None, :, None, None]
            - virt_energy[None, None, None, :]
        )

    def spread(tbar, full):
        return jnp.dot(
            tbar.astype(jnp.bfloat16).reshape(occ * rows, occ * virt),
            full.reshape(occ * virt, aux),
            preferred_element_type=jnp.float32,
        ).reshape(occ, rows, aux)

    diag = pairs(three_index, own_full)
    first = pairs(three_index, part_full)
    second = pairs(part_rows, own_full)
    own = spread(
        (2.0 * diag - diag.transpose(2, 1, 0, 3)) / denominator(occ_energy, occ_energy), own_full
    )
    own += spread(
        (2.0 * first - second.transpose(2, 1, 0, 3)) / denominator(occ_energy, energy_part),
        part_full,
    )
    partner = spread(
        (2.0 * second - first.transpose(2, 1, 0, 3)) / denominator(energy_part, occ_energy),
        own_full,
    ).astype(jnp.bfloat16)
    partner = shifted(partner, "blk", -1)
    return (own + partner.astype(jnp.float32)).astype(jnp.bfloat16)


def kernel(
    blocks,
    a_ref,
    e_ref,
    row_ref,
    o_ref,
    own_full,
    part_full,
    near,
    e_part,
    column_ref,
    tot,
    ptot,
    psend,
    precv,
    hsend,
    hrecv,
    rsend,
    rrecv,
    rel,
    k_ref,
    x_ref,
    d_ref,
    td_ref,
    tu_ref,
    t_ref,
    send_in,
    send_out,
    send_next,
    send_part,
    recv_own,
    recv_part,
    side_sems,
    pass_sems,
    back_sems,
    help_sems,
    result_sems,
    rel_sems,
    e_sems,
    local_sem,
):
    occ, rows, aux = a_ref.shape
    size = occ * rows
    high = rows // STRIPS
    cuts = STRIPS * occ
    turn = cuts // 8
    direct = cuts // 2
    parts = aux // SEND_COLUMNS
    chunks = range(parts)
    v = lax.axis_index("virt")
    g = lax.axis_index("blk")
    copy = lax.axis_index("copies")
    other = 1 - copy
    after = lax.rem(g + 1, blocks)
    before = lax.rem(g + blocks - 1, blocks)
    middle = (v == 1) | (v == 2)
    end = (v == 0) | (v == 3)
    even = lax.rem(g, 2) == 0
    full = copy == 0
    lean = copy == 1
    adj = v + 1 - 2 * lax.rem(v, 2)
    mid = jnp.where(v < 2, 2, 1)
    tip = jnp.where(v < 2, 3, 0)
    inner = jnp.where(middle, mid, adj)
    helper = middle & lean
    served = end & lean
    gathers = jnp.logical_not(served)

    def remote(src, dst, send, recv, **where):
        return pltpu.make_async_remote_copy(
            src_ref=src, dst_ref=dst, send_sem=send, recv_sem=recv,
            device_id=where, device_id_type=MESH,
        )

    def piece(ref, *lead):
        *lead, c = lead
        if isinstance(c, int):
            i, first = c // STRIPS, (c % STRIPS) * high
        else:
            i = lax.div(c, STRIPS)
            first = pl.multiple_of(lax.rem(c, STRIPS) * high, high)
        return ref.at[(*lead, i, pl.ds(first, high))]

    def to_inner(s, c):
        return remote(
            piece(own_full, s, c), piece(own_full, s, c), send_in.at[s, c], recv_own.at[s, c], virt=inner
        )

    def to_outer(s, c):
        return remote(
            piece(own_full, s, c), piece(own_full, s, c), send_out.at[s, c], recv_own.at[s, c], virt=adj
        )

    def to_next(s, c):
        return remote(
            piece(own_full, s, c), piece(part_full, s, c), send_next.at[s, c], recv_part.at[s, c],
            blk=after,
        )

    def part_to_inner(c):
        return remote(
            piece(part_full, v, c), piece(part_full, v, c), send_part.at[c], recv_part.at[v, c],
            virt=adj,
        )

    def own_inner(c):
        return remote(
            piece(a_ref, c), piece(own_full, v, c), send_in.at[v, c], recv_own.at[v, c], virt=inner
        )

    def own_next(c):
        return remote(
            piece(a_ref, c), piece(part_full, v, c), send_next.at[v, c], recv_part.at[v, c], blk=after
        )

    def own_side(c):
        return remote(
            piece(a_ref, c), piece(near, c), side_sems.at[0, c], side_sems.at[1, c], copies=other
        )

    def pass_side(c):
        return remote(
            piece(near, c), piece(own_full, v, c), pass_sems.at[c], recv_own.at[v, c],
            copies=other, virt=adj,
        )

    def back(h, k):
        lines = pl.ds(h * size // 2, size // 2)
        return remote(
            psend.at[k, lines], precv.at[k, lines], back_sems.at[0, h, k], back_sems.at[1, h, k],
            blk=before,
        )

    def help_back(k):
        return remote(
            hsend.at[k], hrecv.at[k], help_sems.at[0, k], help_sems.at[1, k], blk=before
        )

    def help_aside(k):
        return remote(
            hsend.at[k], hsend.at[k], help_sems.at[0, k], help_sems.at[1, k], copies=other
        )

    def pass_help(k):
        return remote(
            hsend.at[k], hrecv.at[k], help_sems.at[0, k], help_sems.at[1, k],
            copies=other, blk=before,
        )

    def by_side(k):
        return k % 2 == 1

    def result(k):
        if by_side(k):
            return remote(
                rsend.at[k], rel.at[k // 2], result_sems.at[0, k], rel_sems.at[0, k // 2], copies=other
            )
        return remote(
            rsend.at[k], rrecv.at[k], result_sems.at[0, k], result_sems.at[1, k], virt=adj
        )

    def pass_result(k):
        return remote(
            rel.at[k // 2], rrecv.at[k], rel_sems.at[1, k // 2], result_sems.at[1, k],
            copies=other, virt=adj,
        )

    energy_copy = remote(e_ref, e_part, e_sems.at[0], e_sems.at[1], blk=after)
    keep = pltpu.make_async_copy(a_ref, own_full.at[v], local_sem)

    barrier = pltpu.get_barrier_semaphore()
    pl.semaphore_signal(barrier, inc=1, device_id={"blk": after}, device_id_type=MESH)
    pl.semaphore_signal(barrier, inc=1, device_id={"blk": before}, device_id_type=MESH)
    pl.semaphore_signal(barrier, inc=1, device_id={"virt": adj}, device_id_type=MESH)
    pl.semaphore_signal(barrier, inc=1, device_id={"copies": other, "virt": adj}, device_id_type=MESH)

    @pl.when(middle)
    def _():
        pl.semaphore_signal(barrier, inc=1, device_id={"virt": mid}, device_id_type=MESH)
        pl.semaphore_signal(barrier, inc=1, device_id={"copies": other}, device_id_type=MESH)
        pl.semaphore_signal(barrier, inc=1, device_id={"copies": other, "blk": after}, device_id_type=MESH)

    pl.semaphore_wait(barrier, 4 + 3 * middle.astype(jnp.int32))

    for c in range(cuts):
        own_inner(c).start()

        @pl.when(middle & full)
        def _():
            own_side(c).start()

    energy_copy.start()
    for c in range(cuts):
        own_next(c).start()
    keep.start()
    for s in range(4):
        column_ref[s] = jnp.transpose(jnp.broadcast_to(row_ref[s], (rows, rows)))[:, 0:1]
    for w in range(2):
        @pl.loop(0, aux // SEND_COLUMNS)
        def _(k):
            cols = pl.ds(pl.multiple_of(k * SEND_COLUMNS, SEND_COLUMNS), SEND_COLUMNS)
            tot[w, :, cols] = jnp.zeros((size, SEND_COLUMNS), jnp.float32)
            ptot[w, :, cols] = jnp.zeros((size, SEND_COLUMNS), jnp.float32)

    keep.wait()

    def inverse(left, i, right, j, r, s):
        return 1.0 / (
            (left[0:1, i : i + 1] + right[0:1, j : j + 1]) - column_ref[r] - row_ref[s]
        )

    def at(i):
        return slice(i * rows, (i + 1) * rows)

    def product(left, source, s, cols, width):
        return jnp.dot(
            left[...], source[s, :, :, cols].reshape(size, width),
            preferred_element_type=jnp.float32,
        )

    def add_columns(total, w, left, source, s):
        @pl.loop(0, aux // SUM_COLUMNS)
        def _(k):
            cols = pl.ds(pl.multiple_of(k * SUM_COLUMNS, SUM_COLUMNS), SUM_COLUMNS)
            total[w, :, cols] += product(left, source, s, cols, SUM_COLUMNS)

    def shard(source, s):
        return source[s].reshape(size, aux)

    def part_arrives(s):
        for c in range(cuts):
            to_next(s, c).wait_recv()

    def pair_ratio(r, s):
        k_ref[...] = contract(shard(own_full, r), shard(own_full, s))
        ratio(k_ref, r, s)

    def ratio(pairs, r, s):
        for i in range(occ):
            for j in range(occ):
                td_ref[at(i), at(j)] = (
                    (2.0 * pairs[at(i), at(j)] - pairs[at(j), at(i)])
                    * inverse(e_ref, i, e_ref, j, r, s)
                ).astype(jnp.bfloat16)

    def diagonal(r, s, w):
        pair_ratio(r, s)
        add_columns(tot, w, td_ref, own_full, s)

    def cross(r, s):
        k_ref[...] = contract(shard(part_full, r), shard(own_full, s))
        x_ref[...] = contract(shard(own_full, r), shard(part_full, s))
        amplitudes(r, s)

    def amplitudes(r, s, own=True, partner=True, blocks=range(occ)):
        for i in range(occ):
            for j in blocks:
                scale = inverse(e_ref, i, e_part, j, r, s)
                x = x_ref[at(i), at(j)]
                y = k_ref[at(j), at(i)]
                if own:
                    t_ref[at(i), at(j)] = ((2.0 * x - y) * scale).astype(jnp.bfloat16)
                if partner:
                    tu_ref[at(j), at(i)] = ((2.0 * y - x) * scale).astype(jnp.bfloat16)

    def spread(s, w):
        add_columns(ptot, w, tu_ref, own_full, s)
        add_columns(tot, w, t_ref, part_full, s)

    def first_half(c):
        @pl.when(gathers)
        def _():
            to_inner(mid, c).wait_recv()

            @pl.when(middle & full)
            def _():
                to_outer(mid, c).start()

            to_next(mid, c).start()

            @pl.when(middle)
            def _():
                to_inner(adj, c).wait_recv()
                to_inner(adj, c).start()

                @pl.when(even | (c < direct))
                def _():
                    to_next(adj, c).start()

            @pl.when(helper)
            def _():
                own_side(c).wait_recv()
                pass_side(c).start()

            @pl.when(end)
            def _():
                to_inner(adj, c).wait_recv()
                to_next(adj, c).start()

    def second_half(c):
        to_inner(tip, c).wait_recv()

        @pl.when(middle)
        def _():
            to_outer(tip, c).start()

        to_next(tip, c).start()

    def send_help(n):
        k = lax.rem(n + parts - ASIDE, parts)
        cols = pl.ds(pl.multiple_of(k * SEND_COLUMNS, SEND_COLUMNS), SEND_COLUMNS)
        hsend[k] = ptot[1, :, cols].astype(jnp.bfloat16)

        @pl.when(even & (n < ASIDE))
        def _():
            help_aside(k).start()

        @pl.when(jnp.logical_not(even & (n < ASIDE)))
        def _():
            help_back(k).start()

    def relay_help(first, last):
        @pl.when(middle & full & even)
        def _():
            for k in range(parts - ASIDE + first, parts - ASIDE + last):
                help_aside(k).wait_recv()
                pass_help(k).start()

    def send_result(k):
        cols = slice(k * SEND_COLUMNS, (k + 1) * SEND_COLUMNS)
        help_back(k).wait_recv()
        rsend[k] = (tot[1, :, cols] + hrecv[k].astype(jnp.float32)).astype(jnp.bfloat16)
        result(k).start()

    def advance(handle, first, last):
        @pl.loop(first * turn, last * turn)
        def _(c):
            handle(c)

    pair_ratio(v, v)
    advance(first_half, 0, 1)
    add_columns(tot, 0, td_ref, own_full, v)
    energy_copy.wait_recv()
    advance(first_half, 1, 3)
    part_arrives(v)

    @pl.when(end & even)
    def _():
        for c in range(direct, cuts):
            part_to_inner(c).start()

    advance(first_half, 3, 4)
    cross(v, v)
    advance(first_half, 4, 5)
    spread(v, 0)
    advance(first_half, 5, 8)
    def paced(t, place):
        count = 0
        for index, sent in enumerate(PACE):
            count = jnp.where(3 * t + place >= 8 + index, sent, count)
        return jnp.where(helper, count, 0)

    def help_until(t, place):
        @pl.loop(paced(t, place - 1), paced(t, place))
        def _(k):
            send_help(k)

    steps = jnp.where(helper, 5, jnp.where(full, 3, 1))

    @pl.loop(1, steps)
    def _(t):
        assist = helper & (t < 3)
        r = jnp.where(assist, adj, v)
        s = jnp.where(
            helper, jnp.where(t == 2, v, jnp.where(t == 4, adj, mid)), jnp.where(t == 1, mid, adj)
        )
        w = assist.astype(jnp.int32)
        pairs = jnp.where(assist, jnp.where(t == 1, 2, 0), 1)

        @pl.loop(0, pairs)
        def _(d):
            diagonal(r, jnp.where(d == 1, v, s), w)

        advance(second_half, 2 * t - 2, 2 * t - 1)
        help_until(t, 0)

        @pl.when(t == 1)
        def _():
            part_arrives(mid)

        @pl.when(t == jnp.where(helper, 1, 2))
        def _():
            part_arrives(adj)

        cross(r, s)
        advance(second_half, 2 * t - 1, 2 * t)
        help_until(t, 1)
        spread(s, w)
        help_until(t, 2)

    ticks = 2 * steps - 2
    advance(second_half, ticks, 6)

    def pairs_with_part(h):
        block = own_full[tip, pl.ds(h * occ // 2, occ // 2)].reshape(size // 2, aux)
        k_ref[:, slice(h * size // 2, (h + 1) * size // 2)] = contract(shard(part_full, v), block)

    def pairs_with_own(h):
        block = own_full[tip, pl.ds(h * occ // 2, occ // 2)].reshape(size // 2, aux)
        d_ref[:, slice(h * size // 2, (h + 1) * size // 2)] = contract(shard(own_full, v), block)

    def part_pairs(h):
        for c in range(h * cuts // 2, (h + 1) * cuts // 2):
            to_next(tip, c).wait_recv()
        block = part_full[tip, pl.ds(h * occ // 2, occ // 2)].reshape(size // 2, aux)
        x_ref[:, slice(h * size // 2, (h + 1) * size // 2)] = contract(shard(own_full, v), block)

    relay_help(0, ASIDE // 2)
    pairs_with_part(0)
    pairs_with_own(0)
    advance(second_half, jnp.maximum(ticks, 6), 7)
    relay_help(ASIDE // 2, ASIDE)
    part_pairs(0)
    advance(second_half, jnp.maximum(ticks, 7), 8)

    @pl.when(helper)
    def _():
        for k in range(READY):
            send_result(k)

    def send_back(h, k):
        cols = slice(k * SEND_COLUMNS, (k + 1) * SEND_COLUMNS)
        lines = slice(h * size // 2, (h + 1) * size // 2)
        psend[k, lines] = (
            ptot[0, lines, cols] + product(tu_ref.at[lines], own_full, tip, cols, SEND_COLUMNS)
        ).astype(jnp.bfloat16)
        back(h, k).start()

    @pl.when(helper)
    def _():
        for k in range(READY, parts):
            send_result(k)

    pairs_with_part(1)
    amplitudes(v, tip, own=False, blocks=range(occ // 2))
    for k in chunks:
        send_back(0, k)
    pairs_with_own(1)
    ratio(d_ref, v, tip)
    part_pairs(1)
    amplitudes(v, tip, own=False, blocks=range(occ // 2, occ))
    for k in chunks:
        send_back(1, k)

        if by_side(k):
            @pl.when(middle & full)
            def _():
                result(k).wait_recv()
                pass_result(k).start()

    amplitudes(v, tip, partner=False)
    add_columns(tot, 0, td_ref, own_full, tip)
    add_columns(tot, 0, t_ref, part_full, tip)

    for k in chunks:
        cols = slice(k * SEND_COLUMNS, (k + 1) * SEND_COLUMNS)

        @pl.when(served)
        def _():
            pass_result(k).wait_recv()
            tot[0, :, cols] += rrecv[k].astype(jnp.float32)

        for h in range(2):
            back(h, k).wait_recv()
        o_ref[:, :, cols] = (
            (tot[0, :, cols] + precv[k].astype(jnp.float32))
            .astype(jnp.bfloat16)
            .reshape(occ, rows, SEND_COLUMNS)
        )

    energy_copy.wait_send()
    for k in chunks:
        for h in range(2):
            back(h, k).wait_send()

    @pl.loop(0, cuts)
    def _(c):
        to_inner(v, c).wait_send()
        to_next(v, c).wait_send()
        to_next(tip, c).wait_send()

        @pl.when(gathers)
        def _():
            to_next(mid, c).wait_send()

        @pl.when(middle)
        def _():
            to_inner(adj, c).wait_send()
            to_outer(tip, c).wait_send()

        @pl.when((middle & (even | (c < direct))) | (end & full))
        def _():
            to_next(adj, c).wait_send()

        @pl.when(middle & full)
        def _():
            to_outer(mid, c).wait_send()
            own_side(c).wait_send()

        @pl.when(helper)
        def _():
            pass_side(c).wait_send()

        @pl.when(end & even & (c >= direct))
        def _():
            part_to_inner(c).wait_send()

    @pl.when(helper)
    def _():
        for k in chunks:
            help_back(k).wait_send()
            result(k).wait_send()

    @pl.when(middle & full)
    def _():
        for k in chunks:
            if by_side(k):
                pass_result(k).wait_send()

    @pl.when(middle & full & even)
    def _():
        for k in range(parts - ASIDE, parts):
            pass_help(k).wait_send()


def fused_local(three_index, occ_energy, virt_energy):
    occ, rows, aux = three_index.shape
    members, blocks = lax.axis_size("virt"), lax.axis_size("blk")
    size, parts = occ * rows, aux // SEND_COLUMNS
    cuts = occ * STRIPS
    vmem = pl.BlockSpec(memory_space=pltpu.VMEM)
    dma = pltpu.SemaphoreType.DMA
    full = pltpu.VMEM((members, occ, rows, aux), jnp.bfloat16)
    total = pltpu.VMEM((2, size, aux), jnp.float32)
    pieces = pltpu.VMEM((parts, size, SEND_COLUMNS), jnp.bfloat16)
    return pl.pallas_call(
        functools.partial(kernel, blocks),
        out_shape=pltpu.VMEM((occ, rows, aux), jnp.bfloat16),
        in_specs=[pl.BlockSpec(memory_space=pl.ANY), vmem, vmem],
        out_specs=vmem,
        scratch_shapes=[
            full,
            full,
            pltpu.VMEM((occ, rows, aux), jnp.bfloat16),
            pltpu.VMEM((1, occ), jnp.float32),
            pltpu.VMEM((members, rows, 1), jnp.float32),
            *[total] * 2,
            *[pieces] * 6,
            pltpu.VMEM((parts // 2, size, SEND_COLUMNS), jnp.bfloat16),
            *[pltpu.VMEM((size, size), jnp.float32)] * 3,
            *[pltpu.VMEM((size, size), jnp.bfloat16)] * 3,
            *[dma((members, cuts))] * 3,
            dma((cuts,)),
            *[dma((members, cuts))] * 2,
            dma((2, cuts)),
            dma((cuts,)),
            dma((2, 2, parts)),
            *[dma((2, parts))] * 2,
            dma((2, parts // 2)),
            dma((2,)),
            dma,
        ],
        compiler_params=pltpu.CompilerParams(
            collective_id=0, has_side_effects=True, vmem_limit_bytes=58 * 2**20
        ),
    )(three_index, occ_energy.reshape(1, occ), virt_energy.reshape(members, 1, rows))


def local(three_index, occ_energy, virt_energy):
    occ, rows, aux = three_index.shape
    tiles = rows % 128 == 0 and aux % SUM_COLUMNS == 0 and occ >= 4
    paired = lax.axis_size("copies") == 2 and lax.axis_size("blk") % 2 == 0
    if tiles and paired and occ % 2 == 0 and lax.axis_size("virt") == 4:
        return fused_local(three_index, occ_energy, virt_energy)
    return plain_local(three_index, occ_energy, virt_energy)


def solution(mesh):
    placed = (P(("copies", "blk"), "virt", None), P(("copies", "blk")), P("copies"))
    return jax.shard_map(
        local,
        mesh=mesh,
        in_specs=placed,
        out_specs=P(("copies", "blk"), "virt", None),
        check_vma=False,
    )
```

```python
import functools

import jax
import jax.numpy as jnp
from jax import lax
from jax.experimental import pallas as pl
from jax.experimental.pallas import tpu as pltpu
from jax.sharding import PartitionSpec as P

MESH = pl.DeviceIdType.MESH
SEND_COLUMNS = 256
SUM_COLUMNS = 1024
STRIPS = 2
READY = 3
ASIDE = 3
PACE = (3, 4, 5, 5, 6, 7, 8)


def shifted(shard, axis, by):
    devices = lax.axis_size(axis)
    return lax.ppermute(shard, axis, [(i, (i + by) % devices) for i in range(devices)])


def contract(left, right):
    return lax.dot_general(
        left, right, (((1,), (1,)), ((), ())), preferred_element_type=jnp.float32
    )


def plain_local(three_index, occ_energy, virt_energy):
    occ, rows, aux = three_index.shape
    virt = virt_energy.shape[0]
    energy_rows = lax.dynamic_slice_in_dim(virt_energy, lax.axis_index("virt") * rows, rows, 0)
    part_rows = shifted(three_index, "blk", 1)
    own_full = lax.all_gather(three_index, "virt", axis=1, tiled=True)
    part_full = shifted(own_full, "blk", 1)
    energy_part = shifted(occ_energy, "blk", 1)

    def pairs(left, right):
        both = contract(left.reshape(occ * rows, aux), right.reshape(occ * virt, aux))
        return both.reshape(occ, rows, occ, virt)

    def denominator(left, right):
        return (
            left[:, None, None, None]
            + right[None, None, :, None]
            - energy_rows[None, :, None, None]
            - virt_energy[None, None, None, :]
        )

    def spread(tbar, full):
        return jnp.dot(
            tbar.astype(jnp.bfloat16).reshape(occ * rows, occ * virt),
            full.reshape(occ * virt, aux),
            preferred_element_type=jnp.float32,
        ).reshape(occ, rows, aux)

    diag = pairs(three_index, own_full)
    first = pairs(three_index, part_full)
    second = pairs(part_rows, own_full)
    own = spread(
        (2.0 * diag - diag.transpose(2, 1, 0, 3)) / denominator(occ_energy, occ_energy), own_full
    )
    own += spread(
        (2.0 * first - second.transpose(2, 1, 0, 3)) / denominator(occ_energy, energy_part),
        part_full,
    )
    partner = spread(
        (2.0 * second - first.transpose(2, 1, 0, 3)) / denominator(energy_part, occ_energy),
        own_full,
    ).astype(jnp.bfloat16)
    partner = shifted(partner, "blk", -1)
    return (own + partner.astype(jnp.float32)).astype(jnp.bfloat16)


def kernel(
    blocks,
    a_ref,
    e_ref,
    row_ref,
    o_ref,
    own_full,
    part_full,
    near,
    e_part,
    column_ref,
    tot,
    ptot,
    psend,
    precv,
    hsend,
    hrecv,
    rsend,
    rrecv,
    rel,
    k_ref,
    x_ref,
    d_ref,
    td_ref,
    tu_ref,
    t_ref,
    send_in,
    send_out,
    send_next,
    send_part,
    recv_own,
    recv_part,
    side_sems,
    pass_sems,
    back_sems,
    help_sems,
    result_sems,
    rel_sems,
    e_sems,
    local_sem,
):
    occ, rows, aux = a_ref.shape
    size = occ * rows
    high = rows // STRIPS
    cuts = STRIPS * occ
    turn = cuts // 8
    direct = cuts // 2
    parts = aux // SEND_COLUMNS
    chunks = range(parts)
    v = lax.axis_index("virt")
    g = lax.axis_index("blk")
    copy = lax.axis_index("copies")
    other = 1 - copy
    after = lax.rem(g + 1, blocks)
    before = lax.rem(g + blocks - 1, blocks)
    middle = (v == 1) | (v == 2)
    end = (v == 0) | (v == 3)
    even = lax.rem(g, 2) == 0
    full = copy == 0
    lean = copy == 1
    adj = v + 1 - 2 * lax.rem(v, 2)
    mid = jnp.where(v < 2, 2, 1)
    tip = jnp.where(v < 2, 3, 0)
    inner = jnp.where(middle, mid, adj)
    helper = middle & lean
    served = end & lean
    gathers = jnp.logical_not(served)

    def remote(src, dst, send, recv, **where):
        return pltpu.make_async_remote_copy(
            src_ref=src, dst_ref=dst, send_sem=send, recv_sem=recv,
            device_id=where, device_id_type=MESH,
        )

    def piece(ref, *lead):
        *lead, c = lead
        if isinstance(c, int):
            i, first = c // STRIPS, (c % STRIPS) * high
        else:
            i = lax.div(c, STRIPS)
            first = pl.multiple_of(lax.rem(c, STRIPS) * high, high)
        return ref.at[(*lead, i, pl.ds(first, high))]

    def to_inner(s, c):
        return remote(
            piece(own_full, s, c), piece(own_full, s, c), send_in.at[s, c], recv_own.at[s, c], virt=inner
        )

    def to_outer(s, c):
        return remote(
            piece(own_full, s, c), piece(own_full, s, c), send_out.at[s, c], recv_own.at[s, c], virt=adj
        )

    def to_next(s, c):
        return remote(
            piece(own_full, s, c), piece(part_full, s, c), send_next.at[s, c], recv_part.at[s, c],
            blk=after,
        )

    def part_to_inner(c):
        return remote(
            piece(part_full, v, c), piece(part_full, v, c), send_part.at[c], recv_part.at[v, c],
            virt=adj,
        )

    def own_inner(c):
        return remote(
            piece(a_ref, c), piece(own_full, v, c), send_in.at[v, c], recv_own.at[v, c], virt=inner
        )

    def own_next(c):
        return remote(
            piece(a_ref, c), piece(part_full, v, c), send_next.at[v, c], recv_part.at[v, c], blk=after
        )

    def own_side(c):
        return remote(
            piece(a_ref, c), piece(near, c), side_sems.at[0, c], side_sems.at[1, c], copies=other
        )

    def pass_side(c):
        return remote(
            piece(near, c), piece(own_full, v, c), pass_sems.at[c], recv_own.at[v, c],
            copies=other, virt=adj,
        )

    def back(h, k):
        lines = pl.ds(h * size // 2, size // 2)
        return remote(
            psend.at[k, lines], precv.at[k, lines], back_sems.at[0, h, k], back_sems.at[1, h, k],
            blk=before,
        )

    def help_back(k):
        return remote(
            hsend.at[k], hrecv.at[k], help_sems.at[0, k], help_sems.at[1, k], blk=before
        )

    def help_aside(k):
        return remote(
            hsend.at[k], hsend.at[k], help_sems.at[0, k], help_sems.at[1, k], copies=other
        )

    def pass_help(k):
        return remote(
            hsend.at[k], hrecv.at[k], help_sems.at[0, k], help_sems.at[1, k],
            copies=other, blk=before,
        )

    def by_side(k):
        return k % 2 == 1 and k < parts - 1

    def result(k):
        if by_side(k):
            return remote(
                rsend.at[k], rel.at[k // 2], result_sems.at[0, k], rel_sems.at[0, k // 2], copies=other
            )
        return remote(
            rsend.at[k], rrecv.at[k], result_sems.at[0, k], result_sems.at[1, k], virt=adj
        )

    def pass_result(k):
        return remote(
            rel.at[k // 2], rrecv.at[k], rel_sems.at[1, k // 2], result_sems.at[1, k],
            copies=other, virt=adj,
        )

    energy_copy = remote(e_ref, e_part, e_sems.at[0], e_sems.at[1], blk=after)
    keep = pltpu.make_async_copy(a_ref, own_full.at[v], local_sem)

    barrier = pltpu.get_barrier_semaphore()
    pl.semaphore_signal(barrier, inc=1, device_id={"blk": after}, device_id_type=MESH)
    pl.semaphore_signal(barrier, inc=1, device_id={"blk": before}, device_id_type=MESH)
    pl.semaphore_signal(barrier, inc=1, device_id={"virt": adj}, device_id_type=MESH)
    pl.semaphore_signal(barrier, inc=1, device_id={"copies": other, "virt": adj}, device_id_type=MESH)

    @pl.when(middle)
    def _():
        pl.semaphore_signal(barrier, inc=1, device_id={"virt": mid}, device_id_type=MESH)
        pl.semaphore_signal(barrier, inc=1, device_id={"copies": other}, device_id_type=MESH)
        pl.semaphore_signal(barrier, inc=1, device_id={"copies": other, "blk": after}, device_id_type=MESH)

    pl.semaphore_wait(barrier, 4 + 3 * middle.astype(jnp.int32))

    for c in range(cuts):
        own_inner(c).start()

        @pl.when(middle & full)
        def _():
            own_side(c).start()

    energy_copy.start()
    for c in range(cuts):
        own_next(c).start()
    keep.start()
    for s in range(4):
        column_ref[s] = jnp.transpose(jnp.broadcast_to(row_ref[s], (rows, rows)))[:, 0:1]
    for w in range(2):
        @pl.loop(0, aux // SEND_COLUMNS)
        def _(k):
            cols = pl.ds(pl.multiple_of(k * SEND_COLUMNS, SEND_COLUMNS), SEND_COLUMNS)
            tot[w, :, cols] = jnp.zeros((size, SEND_COLUMNS), jnp.float32)
            ptot[w, :, cols] = jnp.zeros((size, SEND_COLUMNS), jnp.float32)

    keep.wait()

    def inverse(left, i, right, j, r, s):
        return 1.0 / (
            (left[0:1, i : i + 1] + right[0:1, j : j + 1]) - column_ref[r] - row_ref[s]
        )

    def at(i):
        return slice(i * rows, (i + 1) * rows)

    def product(left, source, s, cols, width):
        return jnp.dot(
            left[...], source[s, :, :, cols].reshape(size, width),
            preferred_element_type=jnp.float32,
        )

    def add_columns(total, w, left, source, s):
        @pl.loop(0, aux // SUM_COLUMNS)
        def _(k):
            cols = pl.ds(pl.multiple_of(k * SUM_COLUMNS, SUM_COLUMNS), SUM_COLUMNS)
            total[w, :, cols] += product(left, source, s, cols, SUM_COLUMNS)

    def shard(source, s):
        return source[s].reshape(size, aux)

    def part_arrives(s):
        for c in range(cuts):
            to_next(s, c).wait_recv()

    def pair_ratio(r, s):
        k_ref[...] = contract(shard(own_full, r), shard(own_full, s))
        ratio(k_ref, r, s)

    def ratio(pairs, r, s):
        for i in range(occ):
            for j in range(occ):
                td_ref[at(i), at(j)] = (
                    (2.0 * pairs[at(i), at(j)] - pairs[at(j), at(i)])
                    * inverse(e_ref, i, e_ref, j, r, s)
                ).astype(jnp.bfloat16)

    def diagonal(r, s, w):
        pair_ratio(r, s)
        add_columns(tot, w, td_ref, own_full, s)

    def cross(r, s):
        k_ref[...] = contract(shard(part_full, r), shard(own_full, s))
        x_ref[...] = contract(shard(own_full, r), shard(part_full, s))
        amplitudes(r, s)

    def amplitudes(r, s, own=True, partner=True, blocks=range(occ)):
        for i in range(occ):
            for j in blocks:
                scale = inverse(e_ref, i, e_part, j, r, s)
                x = x_ref[at(i), at(j)]
                y = k_ref[at(j), at(i)]
                if own:
                    t_ref[at(i), at(j)] = ((2.0 * x - y) * scale).astype(jnp.bfloat16)
                if partner:
                    tu_ref[at(j), at(i)] = ((2.0 * y - x) * scale).astype(jnp.bfloat16)

    def spread(s, w):
        add_columns(ptot, w, tu_ref, own_full, s)
        add_columns(tot, w, t_ref, part_full, s)

    def first_half(c):
        @pl.when(gathers)
        def _():
            to_inner(mid, c).wait_recv()

            @pl.when(middle & full)
            def _():
                to_outer(mid, c).start()

            to_next(mid, c).start()

            @pl.when(middle)
            def _():
                to_inner(adj, c).wait_recv()
                to_inner(adj, c).start()

                @pl.when(even | (c < direct))
                def _():
                    to_next(adj, c).start()

            @pl.when(helper)
            def _():
                own_side(c).wait_recv()
                pass_side(c).start()

            @pl.when(end)
            def _():
                to_inner(adj, c).wait_recv()
                to_next(adj, c).start()

    def second_half(c):
        to_inner(tip, c).wait_recv()

        @pl.when(middle)
        def _():
            to_outer(tip, c).start()

        to_next(tip, c).start()

    def send_help(n):
        k = lax.rem(n + parts - ASIDE, parts)
        cols = pl.ds(pl.multiple_of(k * SEND_COLUMNS, SEND_COLUMNS), SEND_COLUMNS)
        hsend[k] = ptot[1, :, cols].astype(jnp.bfloat16)

        @pl.when(even & (n < ASIDE))
        def _():
            help_aside(k).start()

        @pl.when(jnp.logical_not(even & (n < ASIDE)))
        def _():
            help_back(k).start()

    def relay_help(first, last):
        @pl.when(middle & full & even)
        def _():
            for k in range(parts - ASIDE + first, parts - ASIDE + last):
                help_aside(k).wait_recv()
                pass_help(k).start()

    def send_result(k):
        cols = slice(k * SEND_COLUMNS, (k + 1) * SEND_COLUMNS)
        help_back(k).wait_recv()
        rsend[k] = (tot[1, :, cols] + hrecv[k].astype(jnp.float32)).astype(jnp.bfloat16)
        result(k).start()

    def advance(handle, first, last):
        @pl.loop(first * turn, last * turn)
        def _(c):
            handle(c)

    pair_ratio(v, v)
    advance(first_half, 0, 1)
    add_columns(tot, 0, td_ref, own_full, v)
    energy_copy.wait_recv()
    advance(first_half, 1, 3)
    part_arrives(v)

    @pl.when(end & even)
    def _():
        for c in range(direct, cuts):
            part_to_inner(c).start()

    advance(first_half, 3, 4)
    cross(v, v)
    advance(first_half, 4, 5)
    spread(v, 0)
    advance(first_half, 5, 8)
    def paced(t, place):
        count = 0
        for index, sent in enumerate(PACE):
            count = jnp.where(3 * t + place >= 8 + index, sent, count)
        return jnp.where(helper, count, 0)

    def help_until(t, place):
        @pl.loop(paced(t, place - 1), paced(t, place))
        def _(k):
            send_help(k)

    steps = jnp.where(helper, 5, jnp.where(full, 3, 1))

    @pl.loop(1, steps)
    def _(t):
        assist = helper & (t < 3)
        r = jnp.where(assist, adj, v)
        s = jnp.where(
            helper, jnp.where(t == 2, v, jnp.where(t == 4, adj, mid)), jnp.where(t == 1, mid, adj)
        )
        w = assist.astype(jnp.int32)
        pairs = jnp.where(assist, jnp.where(t == 1, 2, 0), 1)

        @pl.loop(0, pairs)
        def _(d):
            diagonal(r, jnp.where(d == 1, v, s), w)

        advance(second_half, 2 * t - 2, 2 * t - 1)
        help_until(t, 0)

        @pl.when(t == 1)
        def _():
            part_arrives(mid)

        @pl.when(t == jnp.where(helper, 1, 2))
        def _():
            part_arrives(adj)

        cross(r, s)
        advance(second_half, 2 * t - 1, 2 * t)
        help_until(t, 1)
        spread(s, w)
        help_until(t, 2)

    ticks = 2 * steps - 2
    advance(second_half, ticks, 6)

    def pairs_with_part(h):
        block = own_full[tip, pl.ds(h * occ // 2, occ // 2)].reshape(size // 2, aux)
        k_ref[:, slice(h * size // 2, (h + 1) * size // 2)] = contract(shard(part_full, v), block)

    def pairs_with_own(h):
        block = own_full[tip, pl.ds(h * occ // 2, occ // 2)].reshape(size // 2, aux)
        d_ref[:, slice(h * size // 2, (h + 1) * size // 2)] = contract(shard(own_full, v), block)

    def part_pairs(h):
        for c in range(h * cuts // 2, (h + 1) * cuts // 2):
            to_next(tip, c).wait_recv()
        block = part_full[tip, pl.ds(h * occ // 2, occ // 2)].reshape(size // 2, aux)
        x_ref[:, slice(h * size // 2, (h + 1) * size // 2)] = contract(shard(own_full, v), block)

    relay_help(0, ASIDE // 2)
    pairs_with_part(0)
    pairs_with_own(0)
    advance(second_half, jnp.maximum(ticks, 6), 7)
    relay_help(ASIDE // 2, ASIDE)
    part_pairs(0)
    advance(second_half, jnp.maximum(ticks, 7), 8)

    @pl.when(helper)
    def _():
        for k in range(READY):
            send_result(k)

    def send_back(h, k):
        cols = slice(k * SEND_COLUMNS, (k + 1) * SEND_COLUMNS)
        lines = slice(h * size // 2, (h + 1) * size // 2)
        psend[k, lines] = (
            ptot[0, lines, cols] + product(tu_ref.at[lines], own_full, tip, cols, SEND_COLUMNS)
        ).astype(jnp.bfloat16)
        back(h, k).start()

    @pl.when(helper)
    def _():
        for k in range(READY, parts):
            send_result(k)

    pairs_with_part(1)
    amplitudes(v, tip, own=False, blocks=range(occ // 2))
    for k in chunks:
        send_back(0, k)
    pairs_with_own(1)
    ratio(d_ref, v, tip)
    part_pairs(1)
    amplitudes(v, tip, own=False, blocks=range(occ // 2, occ))
    for k in chunks:
        send_back(1, k)

        if by_side(k):
            @pl.when(middle & full)
            def _():
                result(k).wait_recv()
                pass_result(k).start()

    amplitudes(v, tip, partner=False)
    add_columns(tot, 0, td_ref, own_full, tip)
    add_columns(tot, 0, t_ref, part_full, tip)

    for k in chunks:
        cols = slice(k * SEND_COLUMNS, (k + 1) * SEND_COLUMNS)

        @pl.when(served)
        def _():
            pass_result(k).wait_recv()
            tot[0, :, cols] += rrecv[k].astype(jnp.float32)

        for h in range(2):
            back(h, k).wait_recv()
        o_ref[:, :, cols] = (
            (tot[0, :, cols] + precv[k].astype(jnp.float32))
            .astype(jnp.bfloat16)
            .reshape(occ, rows, SEND_COLUMNS)
        )

    energy_copy.wait_send()
    for k in chunks:
        for h in range(2):
            back(h, k).wait_send()

    @pl.loop(0, cuts)
    def _(c):
        to_inner(v, c).wait_send()
        to_next(v, c).wait_send()
        to_next(tip, c).wait_send()

        @pl.when(gathers)
        def _():
            to_next(mid, c).wait_send()

        @pl.when(middle)
        def _():
            to_inner(adj, c).wait_send()
            to_outer(tip, c).wait_send()

        @pl.when((middle & (even | (c < direct))) | (end & full))
        def _():
            to_next(adj, c).wait_send()

        @pl.when(middle & full)
        def _():
            to_outer(mid, c).wait_send()
            own_side(c).wait_send()

        @pl.when(helper)
        def _():
            pass_side(c).wait_send()

        @pl.when(end & even & (c >= direct))
        def _():
            part_to_inner(c).wait_send()

    @pl.when(helper)
    def _():
        for k in chunks:
            help_back(k).wait_send()
            result(k).wait_send()

    @pl.when(middle & full)
    def _():
        for k in chunks:
            if by_side(k):
                pass_result(k).wait_send()

    @pl.when(middle & full & even)
    def _():
        for k in range(parts - ASIDE, parts):
            pass_help(k).wait_send()


def fused_local(three_index, occ_energy, virt_energy):
    occ, rows, aux = three_index.shape
    members, blocks = lax.axis_size("virt"), lax.axis_size("blk")
    size, parts = occ * rows, aux // SEND_COLUMNS
    cuts = occ * STRIPS
    vmem = pl.BlockSpec(memory_space=pltpu.VMEM)
    dma = pltpu.SemaphoreType.DMA
    full = pltpu.VMEM((members, occ, rows, aux), jnp.bfloat16)
    total = pltpu.VMEM((2, size, aux), jnp.float32)
    pieces = pltpu.VMEM((parts, size, SEND_COLUMNS), jnp.bfloat16)
    return pl.pallas_call(
        functools.partial(kernel, blocks),
        out_shape=pltpu.VMEM((occ, rows, aux), jnp.bfloat16),
        in_specs=[pl.BlockSpec(memory_space=pl.ANY), vmem, vmem],
        out_specs=vmem,
        scratch_shapes=[
            full,
            full,
            pltpu.VMEM((occ, rows, aux), jnp.bfloat16),
            pltpu.VMEM((1, occ), jnp.float32),
            pltpu.VMEM((members, rows, 1), jnp.float32),
            *[total] * 2,
            *[pieces] * 6,
            pltpu.VMEM((parts // 2, size, SEND_COLUMNS), jnp.bfloat16),
            *[pltpu.VMEM((size, size), jnp.float32)] * 3,
            *[pltpu.VMEM((size, size), jnp.bfloat16)] * 3,
            *[dma((members, cuts))] * 3,
            dma((cuts,)),
            *[dma((members, cuts))] * 2,
            dma((2, cuts)),
            dma((cuts,)),
            dma((2, 2, parts)),
            *[dma((2, parts))] * 2,
            dma((2, parts // 2)),
            dma((2,)),
            dma,
        ],
        compiler_params=pltpu.CompilerParams(
            collective_id=0, has_side_effects=True, vmem_limit_bytes=58 * 2**20
        ),
    )(three_index, occ_energy.reshape(1, occ), virt_energy.reshape(members, 1, rows))


def local(three_index, occ_energy, virt_energy):
    occ, rows, aux = three_index.shape
    tiles = rows % 128 == 0 and aux % SUM_COLUMNS == 0 and occ >= 4
    paired = lax.axis_size("copies") == 2 and lax.axis_size("blk") % 2 == 0
    if tiles and paired and occ % 2 == 0 and lax.axis_size("virt") == 4:
        return fused_local(three_index, occ_energy, virt_energy)
    return plain_local(three_index, occ_energy, virt_energy)


def solution(mesh):
    placed = (P(("copies", "blk"), "virt", None), P(("copies", "blk")), P("copies"))
    return jax.shard_map(
        local,
        mesh=mesh,
        in_specs=placed,
        out_specs=P(("copies", "blk"), "virt", None),
        check_vma=False,
    )
```

```python
import functools

import jax
import jax.numpy as jnp
from jax import lax
from jax.experimental import pallas as pl
from jax.experimental.pallas import tpu as pltpu
from jax.sharding import PartitionSpec as P

MESH = pl.DeviceIdType.MESH
SEND_COLUMNS = 256
SUM_COLUMNS = 1024
STRIPS = 2
READY = 3
ASIDE = 3
PACE = (3, 4, 5, 5, 6, 7, 8)


def shifted(shard, axis, by):
    devices = lax.axis_size(axis)
    return lax.ppermute(shard, axis, [(i, (i + by) % devices) for i in range(devices)])


def contract(left, right):
    return lax.dot_general(
        left, right, (((1,), (1,)), ((), ())), preferred_element_type=jnp.float32
    )


def plain_local(three_index, occ_energy, virt_energy):
    occ, rows, aux = three_index.shape
    virt = virt_energy.shape[0]
    energy_rows = lax.dynamic_slice_in_dim(virt_energy, lax.axis_index("virt") * rows, rows, 0)
    part_rows = shifted(three_index, "blk", 1)
    own_full = lax.all_gather(three_index, "virt", axis=1, tiled=True)
    part_full = shifted(own_full, "blk", 1)
    energy_part = shifted(occ_energy, "blk", 1)

    def pairs(left, right):
        both = contract(left.reshape(occ * rows, aux), right.reshape(occ * virt, aux))
        return both.reshape(occ, rows, occ, virt)

    def denominator(left, right):
        return (
            left[:, None, None, None]
            + right[None, None, :, None]
            - energy_rows[None, :, None, None]
            - virt_energy[None, None, None, :]
        )

    def spread(tbar, full):
        return jnp.dot(
            tbar.astype(jnp.bfloat16).reshape(occ * rows, occ * virt),
            full.reshape(occ * virt, aux),
            preferred_element_type=jnp.float32,
        ).reshape(occ, rows, aux)

    diag = pairs(three_index, own_full)
    first = pairs(three_index, part_full)
    second = pairs(part_rows, own_full)
    own = spread(
        (2.0 * diag - diag.transpose(2, 1, 0, 3)) / denominator(occ_energy, occ_energy), own_full
    )
    own += spread(
        (2.0 * first - second.transpose(2, 1, 0, 3)) / denominator(occ_energy, energy_part),
        part_full,
    )
    partner = spread(
        (2.0 * second - first.transpose(2, 1, 0, 3)) / denominator(energy_part, occ_energy),
        own_full,
    ).astype(jnp.bfloat16)
    partner = shifted(partner, "blk", -1)
    return (own + partner.astype(jnp.float32)).astype(jnp.bfloat16)


def kernel(
    blocks,
    a_ref,
    e_ref,
    row_ref,
    o_ref,
    own_full,
    part_full,
    near,
    e_part,
    column_ref,
    tot,
    ptot,
    psend,
    precv,
    hsend,
    hrecv,
    rsend,
    rrecv,
    rel,
    k_ref,
    x_ref,
    d_ref,
    td_ref,
    tu_ref,
    t_ref,
    send_in,
    send_out,
    send_next,
    send_part,
    recv_own,
    recv_part,
    side_sems,
    pass_sems,
    back_sems,
    help_sems,
    result_sems,
    rel_sems,
    e_sems,
    local_sem,
):
    occ, rows, aux = a_ref.shape
    size = occ * rows
    high = rows // STRIPS
    cuts = STRIPS * occ
    turn = cuts // 8
    direct = cuts // 2
    parts = aux // SEND_COLUMNS
    chunks = range(parts)
    v = lax.axis_index("virt")
    g = lax.axis_index("blk")
    copy = lax.axis_index("copies")
    other = 1 - copy
    after = lax.rem(g + 1, blocks)
    before = lax.rem(g + blocks - 1, blocks)
    middle = (v == 1) | (v == 2)
    end = (v == 0) | (v == 3)
    even = lax.rem(g, 2) == 0
    full = copy == 0
    lean = copy == 1
    adj = v + 1 - 2 * lax.rem(v, 2)
    mid = jnp.where(v < 2, 2, 1)
    tip = jnp.where(v < 2, 3, 0)
    inner = jnp.where(middle, mid, adj)
    helper = middle & lean
    served = end & lean
    gathers = jnp.logical_not(served)

    def remote(src, dst, send, recv, **where):
        return pltpu.make_async_remote_copy(
            src_ref=src, dst_ref=dst, send_sem=send, recv_sem=recv,
            device_id=where, device_id_type=MESH,
        )

    def piece(ref, *lead):
        *lead, c = lead
        if isinstance(c, int):
            i, first = c // STRIPS, (c % STRIPS) * high
        else:
            i = lax.div(c, STRIPS)
            first = pl.multiple_of(lax.rem(c, STRIPS) * high, high)
        return ref.at[(*lead, i, pl.ds(first, high))]

    def to_inner(s, c):
        return remote(
            piece(own_full, s, c), piece(own_full, s, c), send_in.at[s, c], recv_own.at[s, c], virt=inner
        )

    def to_outer(s, c):
        return remote(
            piece(own_full, s, c), piece(own_full, s, c), send_out.at[s, c], recv_own.at[s, c], virt=adj
        )

    def to_next(s, c):
        return remote(
            piece(own_full, s, c), piece(part_full, s, c), send_next.at[s, c], recv_part.at[s, c],
            blk=after,
        )

    def part_to_inner(c):
        return remote(
            piece(part_full, v, c), piece(part_full, v, c), send_part.at[c], recv_part.at[v, c],
            virt=adj,
        )

    def own_inner(c):
        return remote(
            piece(a_ref, c), piece(own_full, v, c), send_in.at[v, c], recv_own.at[v, c], virt=inner
        )

    def own_next(c):
        return remote(
            piece(a_ref, c), piece(part_full, v, c), send_next.at[v, c], recv_part.at[v, c], blk=after
        )

    def own_side(c):
        return remote(
            piece(a_ref, c), piece(near, c), side_sems.at[0, c], side_sems.at[1, c], copies=other
        )

    def pass_side(c):
        return remote(
            piece(near, c), piece(own_full, v, c), pass_sems.at[c], recv_own.at[v, c],
            copies=other, virt=adj,
        )

    def back(h, k):
        lines = pl.ds(h * size // 2, size // 2)
        return remote(
            psend.at[k, lines], precv.at[k, lines], back_sems.at[0, h, k], back_sems.at[1, h, k],
            blk=before,
        )

    def help_back(k):
        return remote(
            hsend.at[k], hrecv.at[k], help_sems.at[0, k], help_sems.at[1, k], blk=before
        )

    def help_aside(k):
        return remote(
            hsend.at[k], hsend.at[k], help_sems.at[0, k], help_sems.at[1, k], copies=other
        )

    def pass_help(k):
        return remote(
            hsend.at[k], hrecv.at[k], help_sems.at[0, k], help_sems.at[1, k],
            copies=other, blk=before,
        )

    def by_side(k):
        return k % 2 == 1 and k < parts - 1

    def result(k):
        if by_side(k):
            return remote(
                rsend.at[k], rel.at[k // 2], result_sems.at[0, k], rel_sems.at[0, k // 2], copies=other
            )
        return remote(
            rsend.at[k], rrecv.at[k], result_sems.at[0, k], result_sems.at[1, k], virt=adj
        )

    def pass_result(k):
        return remote(
            rel.at[k // 2], rrecv.at[k], rel_sems.at[1, k // 2], result_sems.at[1, k],
            copies=other, virt=adj,
        )

    energy_copy = remote(e_ref, e_part, e_sems.at[0], e_sems.at[1], blk=after)
    keep = pltpu.make_async_copy(a_ref, own_full.at[v], local_sem)

    barrier = pltpu.get_barrier_semaphore()
    pl.semaphore_signal(barrier, inc=1, device_id={"blk": after}, device_id_type=MESH)
    pl.semaphore_signal(barrier, inc=1, device_id={"blk": before}, device_id_type=MESH)
    pl.semaphore_signal(barrier, inc=1, device_id={"virt": adj}, device_id_type=MESH)

    @pl.when(middle)
    def _():
        pl.semaphore_signal(barrier, inc=1, device_id={"virt": mid}, device_id_type=MESH)
        pl.semaphore_signal(barrier, inc=1, device_id={"copies": other}, device_id_type=MESH)
        pl.semaphore_signal(barrier, inc=1, device_id={"copies": other, "blk": after}, device_id_type=MESH)

    pl.semaphore_wait(barrier, 3 + 3 * middle.astype(jnp.int32))

    for c in range(cuts):
        own_inner(c).start()

        @pl.when(middle & full)
        def _():
            own_side(c).start()

    energy_copy.start()
    for c in range(cuts):
        own_next(c).start()
    keep.start()
    for s in range(4):
        column_ref[s] = jnp.transpose(jnp.broadcast_to(row_ref[s], (rows, rows)))[:, 0:1]
    for w in range(2):
        @pl.loop(0, aux // SEND_COLUMNS)
        def _(k):
            cols = pl.ds(pl.multiple_of(k * SEND_COLUMNS, SEND_COLUMNS), SEND_COLUMNS)
            tot[w, :, cols] = jnp.zeros((size, SEND_COLUMNS), jnp.float32)
            ptot[w, :, cols] = jnp.zeros((size, SEND_COLUMNS), jnp.float32)

    keep.wait()

    def inverse(left, i, right, j, r, s):
        return 1.0 / (
            (left[0:1, i : i + 1] + right[0:1, j : j + 1]) - column_ref[r] - row_ref[s]
        )

    def at(i):
        return slice(i * rows, (i + 1) * rows)

    def product(left, source, s, cols, width):
        return jnp.dot(
            left[...], source[s, :, :, cols].reshape(size, width),
            preferred_element_type=jnp.float32,
        )

    def add_columns(total, w, left, source, s):
        @pl.loop(0, aux // SUM_COLUMNS)
        def _(k):
            cols = pl.ds(pl.multiple_of(k * SUM_COLUMNS, SUM_COLUMNS), SUM_COLUMNS)
            total[w, :, cols] += product(left, source, s, cols, SUM_COLUMNS)

    def shard(source, s):
        return source[s].reshape(size, aux)

    def part_arrives(s):
        for c in range(cuts):
            to_next(s, c).wait_recv()

    def pair_ratio(r, s):
        k_ref[...] = contract(shard(own_full, r), shard(own_full, s))
        ratio(k_ref, r, s)

    def ratio(pairs, r, s):
        for i in range(occ):
            for j in range(occ):
                td_ref[at(i), at(j)] = (
                    (2.0 * pairs[at(i), at(j)] - pairs[at(j), at(i)])
                    * inverse(e_ref, i, e_ref, j, r, s)
                ).astype(jnp.bfloat16)

    def diagonal(r, s, w):
        pair_ratio(r, s)
        add_columns(tot, w, td_ref, own_full, s)

    def cross(r, s):
        k_ref[...] = contract(shard(part_full, r), shard(own_full, s))
        x_ref[...] = contract(shard(own_full, r), shard(part_full, s))
        amplitudes(r, s)

    def amplitudes(r, s, own=True, partner=True, blocks=range(occ)):
        for i in range(occ):
            for j in blocks:
                scale = inverse(e_ref, i, e_part, j, r, s)
                x = x_ref[at(i), at(j)]
                y = k_ref[at(j), at(i)]
                if own:
                    t_ref[at(i), at(j)] = ((2.0 * x - y) * scale).astype(jnp.bfloat16)
                if partner:
                    tu_ref[at(j), at(i)] = ((2.0 * y - x) * scale).astype(jnp.bfloat16)

    def spread(s, w):
        add_columns(ptot, w, tu_ref, own_full, s)
        add_columns(tot, w, t_ref, part_full, s)

    def first_half(c):
        @pl.when(gathers)
        def _():
            to_inner(mid, c).wait_recv()

            @pl.when(middle & full)
            def _():
                to_outer(mid, c).start()

            to_next(mid, c).start()

            @pl.when(middle)
            def _():
                to_inner(adj, c).wait_recv()
                to_inner(adj, c).start()

                @pl.when(even | (c < direct))
                def _():
                    to_next(adj, c).start()

            @pl.when(helper)
            def _():
                own_side(c).wait_recv()
                pass_side(c).start()

            @pl.when(end)
            def _():
                to_inner(adj, c).wait_recv()
                to_next(adj, c).start()

    def second_half(c):
        to_inner(tip, c).wait_recv()

        @pl.when(middle)
        def _():
            to_outer(tip, c).start()

        to_next(tip, c).start()

    def send_help(n):
        k = lax.rem(n + parts - ASIDE, parts)
        cols = pl.ds(pl.multiple_of(k * SEND_COLUMNS, SEND_COLUMNS), SEND_COLUMNS)
        hsend[k] = ptot[1, :, cols].astype(jnp.bfloat16)

        @pl.when(even & (n < ASIDE))
        def _():
            help_aside(k).start()

        @pl.when(jnp.logical_not(even & (n < ASIDE)))
        def _():
            help_back(k).start()

    def relay_help(first, last):
        @pl.when(middle & full & even)
        def _():
            for k in range(parts - ASIDE + first, parts - ASIDE + last):
                help_aside(k).wait_recv()
                pass_help(k).start()

    def send_result(k):
        cols = slice(k * SEND_COLUMNS, (k + 1) * SEND_COLUMNS)
        help_back(k).wait_recv()
        rsend[k] = (tot[1, :, cols] + hrecv[k].astype(jnp.float32)).astype(jnp.bfloat16)
        result(k).start()

    def advance(handle, first, last):
        @pl.loop(first * turn, last * turn)
        def _(c):
            handle(c)

    pair_ratio(v, v)
    advance(first_half, 0, 1)
    add_columns(tot, 0, td_ref, own_full, v)
    energy_copy.wait_recv()
    advance(first_half, 1, 3)
    part_arrives(v)

    @pl.when(end & even)
    def _():
        for c in range(direct, cuts):
            part_to_inner(c).start()

    advance(first_half, 3, 4)
    cross(v, v)
    advance(first_half, 4, 5)
    spread(v, 0)
    advance(first_half, 5, 8)
    def paced(t, place):
        count = 0
        for index, sent in enumerate(PACE):
            count = jnp.where(3 * t + place >= 8 + index, sent, count)
        return jnp.where(helper, count, 0)

    def help_until(t, place):
        @pl.loop(paced(t, place - 1), paced(t, place))
        def _(k):
            send_help(k)

    steps = jnp.where(helper, 5, jnp.where(full, 3, 1))

    @pl.loop(1, steps)
    def _(t):
        assist = helper & (t < 3)
        r = jnp.where(assist, adj, v)
        s = jnp.where(
            helper, jnp.where(t == 2, v, jnp.where(t == 4, adj, mid)), jnp.where(t == 1, mid, adj)
        )
        w = assist.astype(jnp.int32)
        pairs = jnp.where(assist, jnp.where(t == 1, 2, 0), 1)

        @pl.loop(0, pairs)
        def _(d):
            diagonal(r, jnp.where(d == 1, v, s), w)

        advance(second_half, 2 * t - 2, 2 * t - 1)
        help_until(t, 0)

        @pl.when(t == 1)
        def _():
            part_arrives(mid)

        @pl.when(t == jnp.where(helper, 1, 2))
        def _():
            part_arrives(adj)

        cross(r, s)
        advance(second_half, 2 * t - 1, 2 * t)
        help_until(t, 1)
        spread(s, w)
        help_until(t, 2)

    ticks = 2 * steps - 2
    advance(second_half, ticks, 6)

    def pairs_with_part(h):
        block = own_full[tip, pl.ds(h * occ // 2, occ // 2)].reshape(size // 2, aux)
        k_ref[:, slice(h * size // 2, (h + 1) * size // 2)] = contract(shard(part_full, v), block)

    def pairs_with_own(h):
        block = own_full[tip, pl.ds(h * occ // 2, occ // 2)].reshape(size // 2, aux)
        d_ref[:, slice(h * size // 2, (h + 1) * size // 2)] = contract(shard(own_full, v), block)

    def part_pairs(h):
        for c in range(h * cuts // 2, (h + 1) * cuts // 2):
            to_next(tip, c).wait_recv()
        block = part_full[tip, pl.ds(h * occ // 2, occ // 2)].reshape(size // 2, aux)
        x_ref[:, slice(h * size // 2, (h + 1) * size // 2)] = contract(shard(own_full, v), block)

    relay_help(0, ASIDE // 2)
    pairs_with_part(0)
    pairs_with_own(0)
    advance(second_half, jnp.maximum(ticks, 6), 7)
    relay_help(ASIDE // 2, ASIDE)
    part_pairs(0)
    advance(second_half, jnp.maximum(ticks, 7), 8)

    @pl.when(helper)
    def _():
        for k in range(READY):
            send_result(k)

    def send_back(h, k):
        cols = slice(k * SEND_COLUMNS, (k + 1) * SEND_COLUMNS)
        lines = slice(h * size // 2, (h + 1) * size // 2)
        psend[k, lines] = (
            ptot[0, lines, cols] + product(tu_ref.at[lines], own_full, tip, cols, SEND_COLUMNS)
        ).astype(jnp.bfloat16)
        back(h, k).start()

    @pl.when(helper)
    def _():
        for k in range(READY, parts):
            send_result(k)

    pairs_with_part(1)
    amplitudes(v, tip, own=False, blocks=range(occ // 2))
    for k in chunks:
        send_back(0, k)
    pairs_with_own(1)
    ratio(d_ref, v, tip)
    part_pairs(1)
    amplitudes(v, tip, own=False, blocks=range(occ // 2, occ))
    for k in chunks:
        send_back(1, k)

        if by_side(k):
            @pl.when(middle & full)
            def _():
                result(k).wait_recv()
                pass_result(k).start()

    amplitudes(v, tip, partner=False)
    add_columns(tot, 0, td_ref, own_full, tip)
    add_columns(tot, 0, t_ref, part_full, tip)

    for k in chunks:
        cols = slice(k * SEND_COLUMNS, (k + 1) * SEND_COLUMNS)

        @pl.when(served)
        def _():
            pass_result(k).wait_recv()
            tot[0, :, cols] += rrecv[k].astype(jnp.float32)

        for h in range(2):
            back(h, k).wait_recv()
        o_ref[:, :, cols] = (
            (tot[0, :, cols] + precv[k].astype(jnp.float32))
            .astype(jnp.bfloat16)
            .reshape(occ, rows, SEND_COLUMNS)
        )

    energy_copy.wait_send()
    for k in chunks:
        for h in range(2):
            back(h, k).wait_send()

    @pl.loop(0, cuts)
    def _(c):
        to_inner(v, c).wait_send()
        to_next(v, c).wait_send()
        to_next(tip, c).wait_send()

        @pl.when(gathers)
        def _():
            to_next(mid, c).wait_send()

        @pl.when(middle)
        def _():
            to_inner(adj, c).wait_send()
            to_outer(tip, c).wait_send()

        @pl.when((middle & (even | (c < direct))) | (end & full))
        def _():
            to_next(adj, c).wait_send()

        @pl.when(middle & full)
        def _():
            to_outer(mid, c).wait_send()
            own_side(c).wait_send()

        @pl.when(helper)
        def _():
            pass_side(c).wait_send()

        @pl.when(end & even & (c >= direct))
        def _():
            part_to_inner(c).wait_send()

    @pl.when(helper)
    def _():
        for k in chunks:
            help_back(k).wait_send()
            result(k).wait_send()

    @pl.when(middle & full)
    def _():
        for k in chunks:
            if by_side(k):
                pass_result(k).wait_send()

    @pl.when(middle & full & even)
    def _():
        for k in range(parts - ASIDE, parts):
            pass_help(k).wait_send()


def fused_local(three_index, occ_energy, virt_energy):
    occ, rows, aux = three_index.shape
    members, blocks = lax.axis_size("virt"), lax.axis_size("blk")
    size, parts = occ * rows, aux // SEND_COLUMNS
    cuts = occ * STRIPS
    vmem = pl.BlockSpec(memory_space=pltpu.VMEM)
    dma = pltpu.SemaphoreType.DMA
    full = pltpu.VMEM((members, occ, rows, aux), jnp.bfloat16)
    total = pltpu.VMEM((2, size, aux), jnp.float32)
    pieces = pltpu.VMEM((parts, size, SEND_COLUMNS), jnp.bfloat16)
    return pl.pallas_call(
        functools.partial(kernel, blocks),
        out_shape=pltpu.VMEM((occ, rows, aux), jnp.bfloat16),
        in_specs=[pl.BlockSpec(memory_space=pl.ANY), vmem, vmem],
        out_specs=vmem,
        scratch_shapes=[
            full,
            full,
            pltpu.VMEM((occ, rows, aux), jnp.bfloat16),
            pltpu.VMEM((1, occ), jnp.float32),
            pltpu.VMEM((members, rows, 1), jnp.float32),
            *[total] * 2,
            *[pieces] * 6,
            pltpu.VMEM((parts // 2, size, SEND_COLUMNS), jnp.bfloat16),
            *[pltpu.VMEM((size, size), jnp.float32)] * 3,
            *[pltpu.VMEM((size, size), jnp.bfloat16)] * 3,
            *[dma((members, cuts))] * 3,
            dma((cuts,)),
            *[dma((members, cuts))] * 2,
            dma((2, cuts)),
            dma((cuts,)),
            dma((2, 2, parts)),
            *[dma((2, parts))] * 2,
            dma((2, parts // 2)),
            dma((2,)),
            dma,
        ],
        compiler_params=pltpu.CompilerParams(
            collective_id=0, has_side_effects=True, vmem_limit_bytes=58 * 2**20
        ),
    )(three_index, occ_energy.reshape(1, occ), virt_energy.reshape(members, 1, rows))


def local(three_index, occ_energy, virt_energy):
    occ, rows, aux = three_index.shape
    tiles = rows % 128 == 0 and aux % SUM_COLUMNS == 0 and occ >= 4
    paired = lax.axis_size("copies") == 2 and lax.axis_size("blk") % 2 == 0
    if tiles and paired and occ % 2 == 0 and lax.axis_size("virt") == 4:
        return fused_local(three_index, occ_energy, virt_energy)
    return plain_local(three_index, occ_energy, virt_energy)


def solution(mesh):
    placed = (P(("copies", "blk"), "virt", None), P(("copies", "blk")), P("copies"))
    return jax.shard_map(
        local,
        mesh=mesh,
        in_specs=placed,
        out_specs=P(("copies", "blk"), "virt", None),
        check_vma=False,
    )
```
